32 devices in a mesh: ia: 4 (over z), ja: 2 (over y), ka: 4 (over x, core).
Axes of the slice: x: 2, y: 2, z: 4, core: 2. Of those that a mesh axis runs over, the one named last changes fastest.
Arguments:
- tile_values: bfloat16 [768, 128], P(('ia', 'ja', 'ka')), may hold values from -0.59765625 to 0.59765625
- tile_rows: int32 [768, 128], P(('ia', 'ja', 'ka')), may hold values from 0 to 63
- tile_cols: int32 [768, 128], P(('ia', 'ja', 'ka')), may hold values from 0 to 2047
- tile_depths: int32 [768, 128], P(('ia', 'ja', 'ka')), may hold values from 0 to 1023
- tile_live: int32 [32, 8], P(('ia', 'ja', 'ka')), may hold values from 0 to 3, as said below
- factor_b: bfloat16 [16, 2, 2048], P(None, 'ja', ('ia', 'ka')), may hold values from -6 to 6
- factor_c: bfloat16 [16, 4, 1024], P(None, 'ka', ('ia', 'ja')), may hold values from -6 to 6
- proj: float32 [16, 256], replicated, may hold values from -0.375 to 0.375
Outputs:
- tucker_y: float32 [2048, 256], P(('ia', 'ja', 'ka'))
- gram: float32 [256, 256], replicated
- new_factor: float32 [16, 2048], P(None, ('ia', 'ja', 'ka'))
The draws below stay inside these ranges and needn't reach their ends.
Inputs may be any that keep to these rules, and one draw needn't show every extreme that they name: tile_live[d, o] counts the live leading slots among the 3 slots that device d holds for the device at index o along ja+ka within its mode-1 block; in every draw there is an owner for which every device has all 3 slots live, and every device has some owner with all 3 slots live.
All inputs are finite; a program needn't handle non-finite values.
Results may differ from the reference program's by a relative error of at most 0.0041.
Values may be sent and summed in bfloat16 or wider, within the bound.
A program may use at most 64 MiB of HBM per device.

```python
import jax
import jax.numpy as jnp
from jax import lax

RANK = 16
KR = 256
TILE = 128
ROWS_DEV = 64
SLOTS = 3
OWNERS = 8
GRID = 32
ALL_TILES = 768
JB = 2048
KB = 1024
N_IA = 4
N_JA = 2
N_KA = 4


def draw_tile_live(key, part):
    base = jax.random.fold_in(key, 31)
    key_level, key_count, key_owner = jax.random.split(base, 3)
    level_row = jax.random.randint(key_level, (GRID, 1), 0, SLOTS)
    drawn = jax.random.randint(key_count, (GRID, OWNERS), 0, SLOTS + 1)
    busy_owner = jax.random.randint(key_owner, (), 0, OWNERS)
    column = jnp.arange(OWNERS, dtype=jnp.int32)[None, :]
    return jnp.where(column == busy_owner, SLOTS, jnp.maximum(drawn, level_row)).astype(jnp.int32)


def place_ends(values, rng, low, largest):
    spot = [jax.random.randint(jax.random.fold_in(rng, axis), (), 0, length) for axis, length in enumerate(values.shape)]
    main_axis = values.shape.index(max(values.shape))
    next_to = spot[:main_axis] + [(spot[main_axis] + 1) % values.shape[main_axis]] + spot[main_axis + 1:]
    return values.at[tuple(spot)].set(low).at[tuple(next_to)].set(largest)


def block_levels(key, dims, shards, least, top_value):
    loudness, own = 1.0, jax.random.fold_in(key, 6)
    for dim, shards_of in shards:
        draws = jnp.exp(jax.random.uniform(jax.random.fold_in(own, dim), (shards_of,), jnp.float32, least / len(shards), top_value / len(shards)))
        loudness = loudness * jnp.repeat(draws, dims[dim] // shards_of).reshape([-1 if axis == dim else 1 for axis in range(len(dims))])
    return loudness


def gaussian(rng, extent, width, reach, pieces=(), held_as=jnp.bfloat16):
    values = jax.random.normal(rng, extent, jnp.float32) * width
    if len(pieces) > 0:
        values = block_levels(rng, extent, pieces, -0.22, 0.18) * values
    return jnp.clip(values, min=-reach, max=reach).astype(held_as)


def setup_inputs(seed: int = 0) -> dict:
    seeds = jax.random.split(jax.random.key(seed), 9)
    return {
        "tile_values": gaussian(seeds[0], (ALL_TILES, TILE), 0.1, 0.59765625, ((0, 32),)),
        "tile_rows": place_ends(jax.random.randint(seeds[1], (ALL_TILES, TILE), 0, ROWS_DEV), jax.random.fold_in(seeds[1], 1), 0, ROWS_DEV - 1).astype(jnp.int32),
        "tile_cols": place_ends(jax.random.randint(seeds[2], (ALL_TILES, TILE), 0, JB), jax.random.fold_in(seeds[2], 1), 0, JB - 1).astype(jnp.int32),
        "tile_depths": place_ends(jax.random.randint(seeds[3], (ALL_TILES, TILE), 0, KB), jax.random.fold_in(seeds[3], 1), 0, KB - 1).astype(jnp.int32),
        "tile_live": draw_tile_live(jax.random.fold_in(seeds[8], 71), 0),
        "factor_b": gaussian(seeds[5], (RANK, N_JA, JB), 1.0, 6.0, ((1, 2), (2, 16))),
        "factor_c": gaussian(seeds[6], (RANK, N_KA, KB), 1.0, 6.0, ((1, 4), (2, 8))),
        "proj": gaussian(seeds[7], (RANK, KR), KR ** -0.5, 0.375, (), jnp.float32),
    }


def reference(tile_values, tile_rows, tile_cols, tile_depths, tile_live, factor_b, factor_c, proj):
    owner_count = N_JA * N_KA
    slot_total = SLOTS * owner_count
    block_rows = ROWS_DEV * owner_count
    total_rows = block_rows * N_IA
    slot_index = jnp.arange(slot_total, dtype=jnp.int32)
    owner_of = slot_index // SLOTS
    place_of = slot_index % SLOTS
    values_all = tile_values.reshape(N_IA * N_JA * N_KA, slot_total, TILE)
    rows_all = tile_rows.reshape(N_IA * N_JA * N_KA, slot_total, TILE)
    cols_all = tile_cols.reshape(N_IA * N_JA * N_KA, slot_total, TILE)
    depths_all = tile_depths.reshape(N_IA * N_JA * N_KA, slot_total, TILE)

    def visit_device(result, device):
        slab_index = device // owner_count
        column_block = (device // N_KA) % N_JA
        depth_block = device % N_KA
        values_here = lax.dynamic_index_in_dim(values_all, device, 0, keepdims=False)
        rows_here = lax.dynamic_index_in_dim(rows_all, device, 0, keepdims=False)
        cols_here = lax.dynamic_index_in_dim(cols_all, device, 0, keepdims=False)
        depths_here = lax.dynamic_index_in_dim(depths_all, device, 0, keepdims=False)
        live_here = lax.dynamic_index_in_dim(tile_live, device, 0, keepdims=False)
        table_b = lax.dynamic_index_in_dim(factor_b, column_block, 1, keepdims=False)
        table_c = lax.dynamic_index_in_dim(factor_c, depth_block, 1, keepdims=False)
        is_live = (place_of < live_here[owner_of]).astype(jnp.float32)
        scaled = (values_here.astype(jnp.float32)[None] * table_b[:, cols_here].astype(jnp.float32)).astype(jnp.bfloat16)
        depth_rows = table_c[:, depths_here]
        kron_rows = (scaled.astype(jnp.float32)[:, None] * depth_rows.astype(jnp.float32)[None, :]).astype(jnp.bfloat16)
        kron_rows = kron_rows.astype(jnp.float32) * is_live[None, None, :, None]
        kron_rows = kron_rows.reshape(RANK * RANK, slot_total * TILE)
        target = slab_index * block_rows + owner_of[:, None] * ROWS_DEV + rows_here
        result = result.at[target.reshape(-1)].add(kron_rows.T)
        return result, None

    start = jnp.zeros((total_rows, RANK * RANK), jnp.float32)
    tucker_y, _ = lax.scan(visit_device, start, jnp.arange(N_IA * N_JA * N_KA, dtype=jnp.int32))
    gram = jnp.dot(tucker_y.T, tucker_y, precision=lax.Precision.HIGHEST, preferred_element_type=jnp.float32) / total_rows
    new_factor = jnp.dot(proj, tucker_y.T, precision=lax.Precision.HIGHEST, preferred_element_type=jnp.float32)
    return (tucker_y, gram, new_factor)
```

```python
import functools

import jax
import jax.numpy as jnp
from jax import lax
from jax.experimental import pallas as pl
from jax.experimental.pallas import tpu as pltpu
from jax.sharding import PartitionSpec as P

ROWS_DEV = 64
LANES = 128
MESH = pl.DeviceIdType.MESH


def repeat(count, body, init):
    if count <= 16:
        for step in range(count):
            init = body(step, init)
        return init
    group = 8

    def turn(index, carry):
        for step in range(group):
            carry = body(index * group + step, carry)
        return carry

    return lax.fori_loop(0, count // group, turn, init)


def lookup(table, index):
    chunks, rank, _ = table.shape
    high = jnp.broadcast_to(index // LANES, (rank, LANES))
    low = jnp.broadcast_to(index % LANES, (rank, LANES))

    def step(chunk, found):
        here = jnp.take_along_axis(table[chunk], low, axis=1, mode="promise_in_bounds")
        return jnp.where(high == chunk, here, found)

    return repeat(chunks, step, jnp.zeros((rank, LANES), jnp.float32))


def kernel(
    n_ia, n_ja, n_ka,
    values, rows, cols, depths, live, fb, fc, proj,
    y_out, gram_out, nf_out,
    values_v, rows_v, cols_v, depths_v, proj_v, live_s, scale_v,
    tb_in, tc_in, tb, tc,
    rows_send, rows_recv, pay_send, pay_recv, kron,
    g_own, g_send, g_recv, z_send, z_recv, final,
    load_sem, tb_ssem, tb_rsem, tc_ssem, tc_rsem, rows_ssem, rows_rsem, pay_ssem, pay_rsem,
    g_ssem, g_rsem, z_ssem, z_rsem, f_ssem, f_rsem,
):
    owners = n_ja * n_ka
    slots = values.shape[0] // owners
    rank = fb.shape[0]
    a, b, c = lax.axis_index("ia"), lax.axis_index("ja"), lax.axis_index("ka")
    me_b = a * n_ka + c
    me_c = a * n_ja + b
    me_o = b * n_ka + c

    loads = []
    for index, (src, dst) in enumerate((
        (values, values_v), (rows, rows_v), (cols, cols_v), (depths, depths_v),
        (proj, proj_v), (live, live_s), (fb, tb_in.at[me_b]), (fc, tc_in.at[me_c]),
    )):
        loads.append(pltpu.make_async_copy(src, dst, load_sem.at[index]))
        loads[-1].start()

    def b_peer(j):
        peer = lax.rem(me_b + j, n_ia * n_ka)
        return (peer // n_ka, b, lax.rem(peer, n_ka))

    def c_peer(j):
        peer = lax.rem(me_c + j, n_ia * n_ja)
        return (peer // n_ja, lax.rem(peer, n_ja), c)

    def o_peer(j):
        peer = lax.rem(me_o + j, owners)
        return (a, peer // n_ka, lax.rem(peer, n_ka))

    def a_peer(j):
        return (lax.rem(a + j, n_ia), b, c)

    barrier = pltpu.get_barrier_semaphore()
    for count, peer in ((n_ia * n_ka, b_peer), (n_ia * n_ja, c_peer), (owners, o_peer)):
        @pl.loop(1, count)
        def _(j, peer=peer):
            pl.semaphore_signal(barrier, inc=1, device_id=peer(j), device_id_type=MESH)
    pl.semaphore_wait(barrier, n_ia * n_ka + n_ia * n_ja + owners - 3)

    def remote(src, dst, ssem, rsem, peer):
        return pltpu.make_async_remote_copy(
            src_ref=src, dst_ref=dst, send_sem=ssem, recv_sem=rsem,
            device_id=peer, device_id_type=MESH,
        )

    def tb_copy(j, slot):
        return remote(fb, tb_in.at[slot], tb_ssem.at[j], tb_rsem.at[slot], b_peer(j))

    def tc_copy(j, slot):
        return remote(fc, tc_in.at[slot], tc_ssem.at[j], tc_rsem.at[slot], c_peer(j))

    @pl.loop(1, n_ia * n_ka)
    def _(j):
        tb_copy(j, me_b).start()

    @pl.loop(1, n_ia * n_ja)
    def _(j):
        tc_copy(j, me_c).start()

    for load in loads:
        load.wait()

    def rows_copy(j, slot):
        return remote(
            rows_send.at[lax.rem(me_o + j, owners)], rows_recv.at[slot],
            rows_ssem.at[j], rows_rsem.at[slot], o_peer(j),
        )

    def pay_copy(j, slot):
        return remote(
            pay_send.at[lax.rem(me_o + j, owners)], pay_recv.at[slot],
            pay_ssem.at[j], pay_rsem.at[slot], o_peer(j),
        )

    @pl.loop(0, owners)
    def _(o):
        for t in range(slots):
            rows_send[o, pl.ds(t, 1), :] = rows_v[pl.ds(o * slots + t, 1), :]

    @pl.loop(1, owners)
    def _(j):
        rows_copy(j, me_o).start()

    scale_v[...] = values_v[...].astype(jnp.float32)
    tb[me_b] = tb_in[me_b].astype(jnp.float32)
    tc[me_c] = tc_in[me_c].astype(jnp.float32)

    @pl.loop(1, n_ia * n_ka)
    def _(j):
        slot = lax.rem(me_b + n_ia * n_ka - j, n_ia * n_ka)
        tb_copy(j, slot).wait_recv()
        tb[slot] = tb_in[slot].astype(jnp.float32)

    @pl.loop(1, n_ia * n_ja)
    def _(j):
        slot = lax.rem(me_c + n_ia * n_ja - j, n_ia * n_ja)
        tc_copy(j, slot).wait_recv()
        tc[slot] = tc_in[slot].astype(jnp.float32)

    def fill(o):
        count = live_s[0, o]
        for t in range(slots):
            row = pl.ds(o * slots + t, 1)
            value = jnp.where(count > t, scale_v[row, :], 0.0)
            pay_send[o, t, pl.ds(0, rank), :] = (lookup(tb, cols_v[row, :]) * value).astype(jnp.bfloat16)
            pay_send[o, t, pl.ds(rank, rank), :] = lookup(tc, depths_v[row, :]).astype(jnp.bfloat16)

    @pl.loop(1, owners)
    def _(j):
        fill(lax.rem(me_o + j, owners))
        pay_copy(j, me_o).start()

    fill(me_o)

    def block(payload, target):
        hot = []
        for t in range(slots):
            part = payload[t].astype(jnp.float32)
            depth = part[rank:]
            for p in range(rank):
                kron[pl.ds(p * rank, rank), pl.ds(t * LANES, LANES)] = (
                    part[p:p + 1] * depth
                ).astype(jnp.bfloat16)
            spot = lax.broadcasted_iota(jnp.int32, (ROWS_DEV, LANES), 0)
            hot.append((target[pl.ds(t, 1), :] == spot).astype(jnp.float32).astype(jnp.bfloat16))
        return lax.dot_general(
            jnp.concatenate(hot, axis=1), kron[...], (((1,), (1,)), ((), ())),
            preferred_element_type=jnp.float32,
        )

    y_out[...] = block(pay_send.at[me_o], rows_send.at[me_o])

    @pl.loop(1, owners)
    def _(j):
        slot = lax.rem(me_o + owners - j, owners)
        rows_copy(j, slot).wait_recv()
        pay_copy(j, slot).wait_recv()
        y_out[...] += block(pay_recv.at[slot], rows_recv.at[slot])

    y = y_out[...]
    gram = lax.dot_general(
        y, y, (((0,), (0,)), ((), ())),
        precision=lax.Precision.HIGHEST, preferred_element_type=jnp.float32,
    ) * (1.0 / (ROWS_DEV * owners * n_ia))
    g_own[...] = gram.reshape(g_own.shape)
    g_send[...] = gram.reshape(g_own.shape).astype(jnp.bfloat16)

    def g_copy(j, slot):
        return remote(
            g_send.at[lax.rem(me_o + j, owners)], g_recv.at[slot],
            g_ssem.at[j], g_rsem.at[slot], o_peer(j),
        )

    @pl.loop(1, owners)
    def _(j):
        g_copy(j, me_o).start()

    nf_out[...] = lax.dot_general(
        proj_v[...], y, (((1,), (1,)), ((), ())),
        precision=lax.Precision.HIGHEST, preferred_element_type=jnp.float32,
    )

    total = g_own[me_o]
    for j in range(1, owners):
        slot = lax.rem(me_o + owners - j, owners)
        g_copy(j, slot).wait_recv()
        total = total + g_recv[slot].astype(jnp.float32)
    z_send[...] = total.astype(jnp.bfloat16)
    z_recv[a] = total.astype(jnp.bfloat16)

    def z_copy(j, slot):
        return remote(z_send, z_recv.at[slot], z_ssem.at[j], z_rsem.at[slot], a_peer(j))

    for j in range(1, n_ia):
        z_copy(j, a).start()
    for j in range(1, n_ia):
        z_copy(j, lax.rem(a + n_ia - j, n_ia)).wait_recv()
    total = z_recv[0].astype(jnp.float32)
    for index in range(1, n_ia):
        total = total + z_recv[index].astype(jnp.float32)
    final[me_o] = total.astype(jnp.bfloat16)

    def f_copy(j, slot):
        return remote(final.at[slot], final.at[slot], f_ssem.at[j], f_rsem.at[slot], o_peer(j))

    height = z_send.shape[0]

    def put(slot):
        start = pl.multiple_of(slot * height, height)
        gram_out[pl.ds(start, height), :] = final[slot].astype(jnp.float32)

    @pl.loop(1, owners)
    def _(j):
        f_copy(j, me_o).start()

    put(me_o)

    @pl.loop(1, owners)
    def _(j):
        slot = lax.rem(me_o + owners - j, owners)
        f_copy(j, slot).wait_recv()
        put(slot)

    @pl.loop(1, n_ia * n_ka)
    def _(j):
        tb_copy(j, me_b).wait_send()

    @pl.loop(1, n_ia * n_ja)
    def _(j):
        tc_copy(j, me_c).wait_send()

    @pl.loop(1, owners)
    def _(j):
        rows_copy(j, me_o).wait_send()
        pay_copy(j, me_o).wait_send()
        g_copy(j, me_o).wait_send()
        f_copy(j, me_o).wait_send()

    for j in range(1, n_ia):
        z_copy(j, a).wait_send()


def on_device(tile_values, tile_rows, tile_cols, tile_depths, tile_live, factor_b, factor_c, proj):
    n_ia, n_ja, n_ka = (lax.axis_size(name) for name in ("ia", "ja", "ka"))
    owners = n_ja * n_ka
    slot_total, tile = tile_values.shape
    slots = slot_total // owners
    rank = factor_b.shape[0]
    columns = proj.shape[1]
    height = columns // owners
    chunks_b, chunks_c = n_ia * n_ka, n_ia * n_ja
    vmem, dma = pltpu.VMEM, pltpu.SemaphoreType.DMA
    f32, bf16, i32 = jnp.float32, jnp.bfloat16, jnp.int32
    return pl.pallas_call(
        functools.partial(kernel, n_ia, n_ja, n_ka),
        out_shape=(
            jax.ShapeDtypeStruct((ROWS_DEV, columns), f32),
            jax.ShapeDtypeStruct((columns, columns), f32),
            jax.ShapeDtypeStruct((rank, ROWS_DEV), f32),
        ),
        in_specs=[pl.BlockSpec(memory_space=pl.ANY)] * 8,
        out_specs=tuple([pl.BlockSpec(memory_space=pltpu.VMEM)] * 3),
        scratch_shapes=[
            vmem((slot_total, tile), bf16),
            vmem((slot_total, tile), i32),
            vmem((slot_total, tile), i32),
            vmem((slot_total, tile), i32),
            vmem(proj.shape, f32),
            pltpu.SMEM((1, owners), i32),
            vmem((slot_total, tile), f32),
            vmem((chunks_b, rank, LANES), bf16),
            vmem((chunks_c, rank, LANES), bf16),
            vmem((chunks_b, rank, LANES), f32),
            vmem((chunks_c, rank, LANES), f32),
            vmem((owners, slots, tile), i32),
            vmem((owners, slots, tile), i32),
            vmem((owners, slots, 2 * rank, tile), bf16),
            vmem((owners, slots, 2 * rank, tile), bf16),
            vmem((columns, slots * tile), bf16),
            vmem((owners, height, columns), f32),
            vmem((owners, height, columns), bf16),
            vmem((owners, height, columns), bf16),
            vmem((height, columns), bf16),
            vmem((n_ia, height, columns), bf16),
            vmem((owners, height, columns), bf16),
            dma((8,)),
            dma((chunks_b,)), dma((chunks_b,)),
            dma((chunks_c,)), dma((chunks_c,)),
            dma((owners,)), dma((owners,)),
            dma((owners,)), dma((owners,)),
            dma((owners,)), dma((owners,)),
            dma((n_ia,)), dma((n_ia,)),
            dma((owners,)), dma((owners,)),
        ],
        compiler_params=pltpu.CompilerParams(collective_id=0, has_side_effects=True),
    )(
        tile_values, tile_rows, tile_cols, tile_depths, tile_live,
        factor_b[:, 0, :], factor_c[:, 0, :], proj,
    )


def solution(mesh):
    return jax.shard_map(
        on_device,
        mesh=mesh,
        in_specs=(
            P(("ia", "ja", "ka"), None),
            P(("ia", "ja", "ka"), None),
            P(("ia", "ja", "ka"), None),
            P(("ia", "ja", "ka"), None),
            P(("ia", "ja", "ka"), None),
            P(None, "ja", ("ia", "ka")),
            P(None, "ka", ("ia", "ja")),
            P(),
        ),
        out_specs=(P(("ia", "ja", "ka"), None), P(), P(None, ("ia", "ja", "ka"))),
        check_vma=False,
    )
```

```python
import functools

import jax
import jax.numpy as jnp
from jax import lax
from jax.experimental import pallas as pl
from jax.experimental.pallas import tpu as pltpu
from jax.sharding import PartitionSpec as P

ROWS_DEV = 64
LANES = 128
MESH = pl.DeviceIdType.MESH


def repeat(count, body, init):
    if count <= 16:
        for step in range(count):
            init = body(step, init)
        return init
    group = 8

    def turn(index, carry):
        for step in range(group):
            carry = body(index * group + step, carry)
        return carry

    return lax.fori_loop(0, count // group, turn, init)


def lookup(table, index):
    chunks, rank, _ = table.shape
    high = jnp.broadcast_to(lax.shift_right_logical(index, LANES.bit_length() - 1), (rank, LANES))
    low = jnp.broadcast_to(index & (LANES - 1), (rank, LANES))

    def step(chunk, found):
        here = jnp.take_along_axis(table[chunk], low, axis=1, mode="promise_in_bounds")
        return jnp.where(high == chunk, here, found)

    return repeat(chunks, step, jnp.zeros((rank, LANES), jnp.float32))


def kernel(
    n_ia, n_ja, n_ka,
    values, rows, cols, depths, live, fb, fc, proj,
    y_out, nf_out, final,
    values_v, rows_v, cols_v, depths_v, proj_v, live_s, scale_v,
    tb_in, tc_in, tb, tc,
    rows_send, rows_recv, pay_send, pay_recv, kron,
    yt_v, g_own, g_send, g_recv, z_send, z_recv,
    load_sem, tb_ssem, tb_rsem, tc_ssem, tc_rsem, rows_ssem, rows_rsem, pay_ssem, pay_rsem,
    g_ssem, g_rsem, z_ssem, z_rsem, f_ssem, f_rsem,
):
    owners = n_ja * n_ka
    slots = values.shape[0] // owners
    rank = fb.shape[0]
    a, b, c = lax.axis_index("ia"), lax.axis_index("ja"), lax.axis_index("ka")
    me_b = a * n_ka + c
    me_c = a * n_ja + b
    me_o = b * n_ka + c

    loads = []
    for index, (src, dst) in enumerate((
        (values, values_v), (rows, rows_v), (cols, cols_v), (depths, depths_v),
        (proj, proj_v), (live, live_s), (fb, tb_in.at[me_b]), (fc, tc_in.at[me_c]),
    )):
        loads.append(pltpu.make_async_copy(src, dst, load_sem.at[index]))
        loads[-1].start()

    def b_peer(j):
        peer = lax.rem(me_b + j, n_ia * n_ka)
        return (peer // n_ka, b, lax.rem(peer, n_ka))

    def c_peer(j):
        peer = lax.rem(me_c + j, n_ia * n_ja)
        return (peer // n_ja, lax.rem(peer, n_ja), c)

    def o_peer(j):
        peer = lax.rem(me_o + j, owners)
        return (a, peer // n_ka, lax.rem(peer, n_ka))

    def a_peer(j):
        return (lax.rem(a + j, n_ia), b, c)

    barrier = pltpu.get_barrier_semaphore()
    for count, peer in ((n_ia * n_ka, b_peer), (n_ia * n_ja, c_peer), (owners, o_peer)):
        @pl.loop(1, count)
        def _(j, peer=peer):
            pl.semaphore_signal(barrier, inc=1, device_id=peer(j), device_id_type=MESH)
    pl.semaphore_wait(barrier, n_ia * n_ka + n_ia * n_ja + owners - 3)

    def remote(src, dst, ssem, rsem, peer):
        return pltpu.make_async_remote_copy(
            src_ref=src, dst_ref=dst, send_sem=ssem, recv_sem=rsem,
            device_id=peer, device_id_type=MESH,
        )

    def tb_copy(j, slot):
        return remote(fb, tb_in.at[slot], tb_ssem.at[j], tb_rsem.at[slot], b_peer(j))

    def tc_copy(j, slot):
        return remote(fc, tc_in.at[slot], tc_ssem.at[j], tc_rsem.at[slot], c_peer(j))

    @pl.loop(1, n_ia * n_ka)
    def _(j):
        tb_copy(j, me_b).start()

    @pl.loop(1, n_ia * n_ja)
    def _(j):
        tc_copy(j, me_c).start()

    for load in loads:
        load.wait()

    def rows_copy(j, slot):
        return remote(
            rows_send.at[lax.rem(me_o + j, owners)], rows_recv.at[slot],
            rows_ssem.at[j], rows_rsem.at[slot], o_peer(j),
        )

    def pay_copy(j, slot):
        return remote(
            pay_send.at[lax.rem(me_o + j, owners)], pay_recv.at[slot],
            pay_ssem.at[j], pay_rsem.at[slot], o_peer(j),
        )

    @pl.loop(0, owners)
    def _(o):
        for t in range(slots):
            rows_send[o, pl.ds(t, 1), :] = rows_v[pl.ds(o * slots + t, 1), :]

    @pl.loop(1, owners)
    def _(j):
        rows_copy(j, me_o).start()

    scale_v[...] = values_v[...].astype(jnp.float32)
    tb[me_b] = tb_in[me_b].astype(jnp.float32)
    tc[me_c] = tc_in[me_c].astype(jnp.float32)

    @pl.loop(1, n_ia * n_ka)
    def _(j):
        slot = lax.rem(me_b + n_ia * n_ka - j, n_ia * n_ka)
        tb_copy(j, slot).wait_recv()
        tb[slot] = tb_in[slot].astype(jnp.float32)

    @pl.loop(1, n_ia * n_ja)
    def _(j):
        slot = lax.rem(me_c + n_ia * n_ja - j, n_ia * n_ja)
        tc_copy(j, slot).wait_recv()
        tc[slot] = tc_in[slot].astype(jnp.float32)

    def fill(o):
        count = live_s[0, o]
        for t in range(slots):
            row = pl.ds(o * slots + t, 1)
            value = jnp.where(count > t, scale_v[row, :], 0.0)
            pay_send[o, t, pl.ds(0, rank), :] = (lookup(tb, cols_v[row, :]) * value).astype(jnp.bfloat16)
            pay_send[o, t, pl.ds(rank, rank), :] = lookup(tc, depths_v[row, :]).astype(jnp.bfloat16)

    @pl.loop(1, owners)
    def _(j):
        fill(lax.rem(me_o + j, owners))
        pay_copy(j, me_o).start()

    fill(me_o)

    def block(payload, target):
        hot = []
        for t in range(slots):
            part = payload[t].astype(jnp.float32)
            depth = part[rank:]
            for p in range(rank):
                kron[pl.ds(p * rank, rank), pl.ds(t * LANES, LANES)] = (
                    part[p:p + 1] * depth
                ).astype(jnp.bfloat16)
            spot = lax.broadcasted_iota(jnp.int32, (ROWS_DEV, LANES), 0)
            hot.append((target[pl.ds(t, 1), :] == spot).astype(jnp.float32).astype(jnp.bfloat16))
        return lax.dot_general(
            kron[...], jnp.concatenate(hot, axis=1), (((1,), (1,)), ((), ())),
            preferred_element_type=jnp.float32,
        )

    yt_v[...] = block(pay_send.at[me_o], rows_send.at[me_o])

    @pl.loop(1, n_ia * n_ka)
    def _(j):
        tb_copy(j, me_b).wait_send()

    @pl.loop(1, n_ia * n_ja)
    def _(j):
        tc_copy(j, me_c).wait_send()

    @pl.loop(1, owners)
    def _(j):
        rows_copy(j, me_o).wait_send()

    @pl.loop(1, owners)
    def _(j):
        slot = lax.rem(me_o + owners - j, owners)
        rows_copy(j, slot).wait_recv()
        pay_copy(j, slot).wait_recv()
        yt_v[...] += block(pay_recv.at[slot], rows_recv.at[slot])

    def g_copy(i, j, slot):
        return remote(
            g_send.at[i, lax.rem(me_o + j, owners)], g_recv.at[i, slot],
            g_ssem.at[i, j], g_rsem.at[i, slot], o_peer(j),
        )

    def z_copy(i, j, slot):
        return remote(z_send.at[i], z_recv.at[i, slot], z_ssem.at[i, j], z_rsem.at[i, slot], a_peer(j))

    def f_copy(i, j, slot):
        return remote(
            final.at[i, slot], final.at[i, slot], f_ssem.at[i, j], f_rsem.at[i, slot], o_peer(j)
        )

    half = kron.shape[0] // 2
    pieces = ((0, 0), (0, 1), (1, 1))
    scale = 1.0 / (ROWS_DEV * owners * n_ia)
    for i, (left, right) in enumerate(pieces):
        piece = lax.dot_general(
            yt_v[pl.ds(left * half, half), :], yt_v[pl.ds(right * half, half), :],
            (((1,), (1,)), ((), ())),
            precision=lax.Precision.HIGHEST, preferred_element_type=jnp.float32,
        ) * scale
        g_own[i] = piece.reshape(g_own.shape[1:])
        g_send[i] = piece.reshape(g_own.shape[1:]).astype(jnp.bfloat16)

        @pl.loop(1, owners)
        def _(j, i=i):
            g_copy(i, j, me_o).start()

    nf_out[...] = lax.dot_general(
        proj_v[...], yt_v[...], (((1,), (0,)), ((), ())),
        precision=lax.Precision.HIGHEST, preferred_element_type=jnp.float32,
    )
    y_out[...] = jnp.transpose(yt_v[...])

    @pl.loop(1, owners)
    def _(j):
        pay_copy(j, me_o).wait_send()

    for i in range(len(pieces)):
        total = g_own[i, me_o]
        for j in range(1, owners):
            slot = lax.rem(me_o + owners - j, owners)
            g_copy(i, j, slot).wait_recv()
            total = total + g_recv[i, slot].astype(jnp.float32)
        z_send[i] = total.astype(jnp.bfloat16)
        z_recv[i, a] = total.astype(jnp.bfloat16)
        for j in range(1, n_ia):
            z_copy(i, j, a).start()

    for i in range(len(pieces)):
        for j in range(1, n_ia):
            z_copy(i, j, lax.rem(a + n_ia - j, n_ia)).wait_recv()
        total = z_recv[i, 0].astype(jnp.float32)
        for index in range(1, n_ia):
            total = total + z_recv[i, index].astype(jnp.float32)
        final[i, me_o] = total.astype(jnp.bfloat16)

        @pl.loop(1, owners)
        def _(j, i=i):
            f_copy(i, j, me_o).start()

    @pl.loop(1, owners)
    def _(j):
        for i in range(len(pieces)):
            g_copy(i, j, me_o).wait_send()

    for i in range(len(pieces)):
        for j in range(1, n_ia):
            z_copy(i, j, a).wait_send()

    @pl.loop(1, owners)
    def _(j):
        for i in range(len(pieces)):
            f_copy(i, j, lax.rem(me_o + owners - j, owners)).wait_recv()

    @pl.loop(1, owners)
    def _(j):
        for i in range(len(pieces)):
            f_copy(i, j, me_o).wait_send()


def finish(y, nf, final, y_out, gram_out, nf_out, gram_v, sem):
    copies = [
        pltpu.make_async_copy(y, y_out, sem.at[0]),
        pltpu.make_async_copy(nf, nf_out, sem.at[1]),
    ]
    for copy in copies:
        copy.start()
    half = gram_v.shape[1] // 2
    blocks = [final[i].astype(jnp.float32).reshape(half, half) for i in range(3)]
    top, bottom = pl.ds(0, half), pl.ds(half, half)
    gram_v[top, top] = blocks[0]
    gram_v[top, bottom] = blocks[1]
    copies.append(pltpu.make_async_copy(gram_v.at[top], gram_out.at[top], sem.at[2]))
    copies[-1].start()
    gram_v[bottom, top] = jnp.transpose(blocks[1])
    gram_v[bottom, bottom] = blocks[2]
    copies.append(pltpu.make_async_copy(gram_v.at[bottom], gram_out.at[bottom], sem.at[3]))
    copies[-1].start()
    for copy in copies:
        copy.wait()


def on_device(tile_values, tile_rows, tile_cols, tile_depths, tile_live, factor_b, factor_c, proj):
    n_ia, n_ja, n_ka = (lax.axis_size(name) for name in ("ia", "ja", "ka"))
    owners = n_ja * n_ka
    slot_total, tile = tile_values.shape
    slots = slot_total // owners
    rank = factor_b.shape[0]
    columns = proj.shape[1]
    half = columns // 2
    height = half // owners
    chunks_b, chunks_c = n_ia * n_ka, n_ia * n_ja
    vmem, dma = pltpu.VMEM, pltpu.SemaphoreType.DMA
    f32, bf16, i32 = jnp.float32, jnp.bfloat16, jnp.int32
    held = pl.pallas_call(
        functools.partial(kernel, n_ia, n_ja, n_ka),
        out_shape=(
            vmem((ROWS_DEV, columns), f32),
            vmem((rank, ROWS_DEV), f32),
            vmem((3, owners, height, half), bf16),
        ),
        in_specs=[pl.BlockSpec(memory_space=pl.ANY)] * 8,
        out_specs=tuple([pl.BlockSpec(memory_space=pltpu.VMEM)] * 3),
        scratch_shapes=[
            vmem((slot_total, tile), bf16),
            vmem((slot_total, tile), i32),
            vmem((slot_total, tile), i32),
            vmem((slot_total, tile), i32),
            vmem(proj.shape, f32),
            pltpu.SMEM((1, owners), i32),
            vmem((slot_total, tile), f32),
            vmem((chunks_b, rank, LANES), bf16),
            vmem((chunks_c, rank, LANES), bf16),
            vmem((chunks_b, rank, LANES), f32),
            vmem((chunks_c, rank, LANES), f32),
            vmem((owners, slots, tile), i32),
            vmem((owners, slots, tile), i32),
            vmem((owners, slots, 2 * rank, tile), bf16),
            vmem((owners, slots, 2 * rank, tile), bf16),
            vmem((columns, slots * tile), bf16),
            vmem((columns, ROWS_DEV), f32),
            vmem((3, owners, height, half), f32),
            vmem((3, owners, height, half), bf16),
            vmem((3, owners, height, half), bf16),
            vmem((3, height, half), bf16),
            vmem((3, n_ia, height, half), bf16),
            dma((8,)),
            dma((chunks_b,)), dma((chunks_b,)),
            dma((chunks_c,)), dma((chunks_c,)),
            dma((owners,)), dma((owners,)),
            dma((owners,)), dma((owners,)),
            dma((3, owners)), dma((3, owners)),
            dma((3, n_ia)), dma((3, n_ia)),
            dma((3, owners)), dma((3, owners)),
        ],
        compiler_params=pltpu.CompilerParams(collective_id=0, has_side_effects=True),
    )(
        tile_values, tile_rows, tile_cols, tile_depths, tile_live,
        factor_b[:, 0, :], factor_c[:, 0, :], proj,
    )
    return pl.pallas_call(
        finish,
        out_shape=(
            jax.ShapeDtypeStruct((ROWS_DEV, columns), f32),
            jax.ShapeDtypeStruct((columns, columns), f32),
            jax.ShapeDtypeStruct((rank, ROWS_DEV), f32),
        ),
        in_specs=[pl.BlockSpec(memory_space=pltpu.VMEM)] * 3,
        out_specs=tuple([pl.BlockSpec(memory_space=pl.ANY)] * 3),
        scratch_shapes=[vmem((columns, columns), f32), dma((4,))],
    )(*(pltpu.with_memory_space_constraint(array, vmem) for array in held))


def solution(mesh):
    return jax.shard_map(
        on_device,
        mesh=mesh,
        in_specs=(
            P(("ia", "ja", "ka"), None),
            P(("ia", "ja", "ka"), None),
            P(("ia", "ja", "ka"), None),
            P(("ia", "ja", "ka"), None),
            P(("ia", "ja", "ka"), None),
            P(None, "ja", ("ia", "ka")),
            P(None, "ka", ("ia", "ja")),
            P(),
        ),
        out_specs=(P(("ia", "ja", "ka"), None), P(), P(None, ("ia", "ja", "ka"))),
        check_vma=False,
    )
```

```python
import functools

import jax
import jax.numpy as jnp
from jax import lax
from jax.experimental import pallas as pl
from jax.experimental.pallas import tpu as pltpu
from jax.sharding import PartitionSpec as P

ROWS_DEV = 64
LANES = 128
MESH = pl.DeviceIdType.MESH


def each(begin, end):
    if end - begin > 16:
        return pl.loop(begin, end)

    def run(body):
        for step in range(begin, end):
            body(step)

    return run


def repeat(count, body, init):
    if count <= 16:
        for step in range(count):
            init = body(step, init)
        return init
    group = 8

    def turn(index, carry):
        for step in range(group):
            carry = body(index * group + step, carry)
        return carry

    return lax.fori_loop(0, count // group, turn, init)


def lookup(table, index):
    chunks, rank, _ = table.shape
    high = jnp.broadcast_to(lax.shift_right_logical(index, LANES.bit_length() - 1), (rank, LANES))
    low = jnp.broadcast_to(index & (LANES - 1), (rank, LANES))

    def step(chunk, found):
        here = jnp.take_along_axis(table[chunk], low, axis=1, mode="promise_in_bounds")
        return jnp.where(high == chunk, here, found)

    return repeat(chunks, step, jnp.zeros((rank, LANES), jnp.float32))


def kernel(
    n_ia, n_ja, n_ka,
    values, rows, cols, depths, live, fb, fc, proj,
    y_out, nf_out, final,
    values_v, rows_v, cols_v, depths_v, proj_v, live_s, scale_v,
    tb_in, tc_in, tb, tc,
    rows_send, rows_recv, pay_send, pay_recv, kron,
    yt_v, g_left, g_right, g_own, g_send, g_recv, z_send, z_recv,
    load_sem, tb_ssem, tb_rsem, tc_ssem, tc_rsem, rows_ssem, rows_rsem, pay_ssem, pay_rsem,
    g_ssem, g_rsem, z_ssem, z_rsem, f_ssem, f_rsem,
):
    owners = n_ja * n_ka
    slots = values.shape[0] // owners
    rank = fb.shape[0]
    a, b, c = lax.axis_index("ia"), lax.axis_index("ja"), lax.axis_index("ka")
    me_b = a * n_ka + c
    me_c = a * n_ja + b
    me_o = b * n_ka + c

    loads = []
    for index, (src, dst) in enumerate((
        (values, values_v), (rows, rows_v), (cols, cols_v), (depths, depths_v),
        (proj, proj_v), (live, live_s), (fb, tb_in.at[me_b]), (fc, tc_in.at[me_c]),
    )):
        loads.append(pltpu.make_async_copy(src, dst, load_sem.at[index]))
        loads[-1].start()

    def b_peer(j):
        peer = lax.rem(me_b + j, n_ia * n_ka)
        return (peer // n_ka, b, lax.rem(peer, n_ka))

    def c_peer(j):
        peer = lax.rem(me_c + j, n_ia * n_ja)
        return (peer // n_ja, lax.rem(peer, n_ja), c)

    def o_peer(j):
        return (a, lax.rem(b + j // n_ka, n_ja), lax.rem(c + j % n_ka, n_ka))

    def to_o(j):
        return lax.rem(b + j // n_ka, n_ja) * n_ka + lax.rem(c + j % n_ka, n_ka)

    def from_o(j):
        return lax.rem(b + n_ja - j // n_ka, n_ja) * n_ka + lax.rem(c + n_ka - j % n_ka, n_ka)

    def a_peer(j):
        return (lax.rem(a + j, n_ia), b, c)

    barrier = pltpu.get_barrier_semaphore()
    for count, peer in ((n_ia * n_ka, b_peer), (n_ia * n_ja, c_peer), (owners, o_peer)):
        @each(1, count)
        def _(j, peer=peer):
            pl.semaphore_signal(barrier, inc=1, device_id=peer(j), device_id_type=MESH)

    for load in loads:
        load.wait()

    @each(0, owners)
    def _(o):
        for t in range(slots):
            rows_send[o, pl.ds(t, 1), :] = rows_v[pl.ds(o * slots + t, 1), :]

    scale_v[...] = values_v[...].astype(jnp.float32)
    tb[me_b] = tb_in[me_b].astype(jnp.float32)
    tc[me_c] = tc_in[me_c].astype(jnp.float32)
    pl.semaphore_wait(barrier, n_ia * n_ka + n_ia * n_ja + owners - 3)

    def remote(src, dst, ssem, rsem, peer):
        return pltpu.make_async_remote_copy(
            src_ref=src, dst_ref=dst, send_sem=ssem, recv_sem=rsem,
            device_id=peer, device_id_type=MESH,
        )

    def tb_copy(j, slot):
        return remote(fb, tb_in.at[slot], tb_ssem.at[j], tb_rsem.at[slot], b_peer(j))

    def tc_copy(j, slot):
        return remote(fc, tc_in.at[slot], tc_ssem.at[j], tc_rsem.at[slot], c_peer(j))

    @each(1, n_ia * n_ka)
    def _(j):
        tb_copy(j, me_b).start()

    @each(1, n_ia * n_ja)
    def _(j):
        tc_copy(j, me_c).start()

    def rows_copy(j, slot):
        return remote(
            rows_send.at[to_o(j)], rows_recv.at[slot],
            rows_ssem.at[j], rows_rsem.at[slot], o_peer(j),
        )

    def pay_copy(j, slot):
        return remote(
            pay_send.at[to_o(j)], pay_recv.at[slot],
            pay_ssem.at[j], pay_rsem.at[slot], o_peer(j),
        )

    @each(1, owners)
    def _(j):
        rows_copy(j, me_o).start()

    @each(1, n_ia * n_ka)
    def _(j):
        slot = lax.rem(me_b + n_ia * n_ka - j, n_ia * n_ka)
        tb_copy(j, slot).wait_recv()
        tb[slot] = tb_in[slot].astype(jnp.float32)

    @each(1, n_ia * n_ja)
    def _(j):
        slot = lax.rem(me_c + n_ia * n_ja - j, n_ia * n_ja)
        tc_copy(j, slot).wait_recv()
        tc[slot] = tc_in[slot].astype(jnp.float32)

    def fill(o):
        count = live_s[0, o]
        for t in range(slots):
            row = pl.ds(o * slots + t, 1)
            value = jnp.where(count > t, scale_v[row, :], 0.0)
            pay_send[o, t, pl.ds(0, rank), :] = (lookup(tb, cols_v[row, :]) * value).astype(jnp.bfloat16)
            pay_send[o, t, pl.ds(rank, rank), :] = lookup(tc, depths_v[row, :]).astype(jnp.bfloat16)

    @pl.loop(1, owners)
    def _(j):
        fill(to_o(owners - j))
        pay_copy(owners - j, me_o).start()

    fill(me_o)

    def block(payload, target):
        hot = []
        for t in range(slots):
            part = payload[t].astype(jnp.float32)
            depth = part[rank:]
            for p in range(rank):
                kron[pl.ds(p * rank, rank), pl.ds(t * LANES, LANES)] = (
                    part[p:p + 1] * depth
                ).astype(jnp.bfloat16)
            spot = lax.broadcasted_iota(jnp.int32, (ROWS_DEV, LANES), 0)
            hot.append((target[pl.ds(t, 1), :] == spot).astype(jnp.float32).astype(jnp.bfloat16))
        return lax.dot_general(
            kron[...], jnp.concatenate(hot, axis=1), (((1,), (1,)), ((), ())),
            preferred_element_type=jnp.float32,
        )

    yt_v[...] = block(pay_send.at[me_o], rows_send.at[me_o])

    @each(1, n_ia * n_ka)
    def _(j):
        tb_copy(j, me_b).wait_send()

    @each(1, n_ia * n_ja)
    def _(j):
        tc_copy(j, me_c).wait_send()

    @each(1, owners)
    def _(j):
        rows_copy(j, me_o).wait_send()

    @pl.loop(1, owners)
    def _(j):
        slot = from_o(j)
        rows_copy(j, slot).wait_recv()
        pay_copy(j, slot).wait_recv()
        yt_v[...] += block(pay_recv.at[slot], rows_recv.at[slot])

    def g_copy(i, j, slot):
        return remote(
            g_send.at[i, to_o(j)], g_recv.at[i, slot],
            g_ssem.at[i, j], g_rsem.at[i, slot], o_peer(j),
        )

    def z_copy(i, j, slot):
        return remote(z_send.at[i], z_recv.at[i, slot], z_ssem.at[i, j], z_rsem.at[i, slot], a_peer(j))

    def f_copy(i, j, slot):
        return remote(
            final.at[i, slot], final.at[i, slot], f_ssem.at[i, j], f_rsem.at[i, slot], o_peer(j)
        )

    half = kron.shape[0] // 2
    pieces = ((0, 0), (0, 1), (1, 1))
    yt = yt_v[...]
    high = yt.astype(jnp.bfloat16).astype(jnp.float32)
    low = yt - high
    g_left[...] = jnp.concatenate([high, low, high, low], axis=1).astype(jnp.bfloat16)
    g_right[...] = jnp.concatenate([high, high, low, low], axis=1).astype(jnp.bfloat16)
    scale = 1.0 / (ROWS_DEV * owners * n_ia)
    for i, (left, right) in enumerate(pieces):
        piece = lax.dot_general(
            g_left[pl.ds(left * half, half), :], g_right[pl.ds(right * half, half), :],
            (((1,), (1,)), ((), ())), preferred_element_type=jnp.float32,
        ) * scale
        g_own[i] = piece.reshape(g_own.shape[1:])
        g_send[i] = piece.reshape(g_own.shape[1:]).astype(jnp.bfloat16)

        @each(1, owners)
        def _(j, i=i):
            g_copy(i, owners - j, me_o).start()

    nf_out[...] = lax.dot_general(
        proj_v[...], yt_v[...], (((1,), (0,)), ((), ())),
        precision=lax.Precision.HIGHEST, preferred_element_type=jnp.float32,
    )
    y_out[...] = jnp.transpose(yt_v[...])

    @each(1, owners)
    def _(j):
        pay_copy(j, me_o).wait_send()

    for i in range(len(pieces)):
        total = g_own[i, me_o]
        for j in range(1, owners):
            slot = from_o(j)
            g_copy(i, j, slot).wait_recv()
            total = total + g_recv[i, slot].astype(jnp.float32)
        z_send[i] = total.astype(jnp.bfloat16)
        z_recv[i, a] = total.astype(jnp.bfloat16)
        for j in range(1, n_ia):
            z_copy(i, j, a).start()

    for i in range(len(pieces)):
        for j in range(1, n_ia):
            z_copy(i, j, lax.rem(a + n_ia - j, n_ia)).wait_recv()
        total = z_recv[i, 0].astype(jnp.float32)
        for index in range(1, n_ia):
            total = total + z_recv[i, index].astype(jnp.float32)
        final[i, me_o] = total.astype(jnp.bfloat16)

        @each(1, owners)
        def _(j, i=i):
            f_copy(i, owners - j, me_o).start()

    @each(1, owners)
    def _(j):
        for i in range(len(pieces)):
            g_copy(i, j, me_o).wait_send()

    for i in range(len(pieces)):
        for j in range(1, n_ia):
            z_copy(i, j, a).wait_send()

    @each(1, owners)
    def _(j):
        for i in range(len(pieces)):
            f_copy(i, j, from_o(j)).wait_recv()

    @each(1, owners)
    def _(j):
        for i in range(len(pieces)):
            f_copy(i, j, me_o).wait_send()


def finish(y, nf, final, y_out, gram_out, nf_out, gram_v, sem):
    copies = [
        pltpu.make_async_copy(y, y_out, sem.at[0]),
        pltpu.make_async_copy(nf, nf_out, sem.at[1]),
    ]
    for copy in copies:
        copy.start()
    half = gram_v.shape[1] // 2
    blocks = [final[i].astype(jnp.float32).reshape(half, half) for i in range(3)]
    top, bottom = pl.ds(0, half), pl.ds(half, half)
    gram_v[top, top] = blocks[0]
    gram_v[top, bottom] = blocks[1]
    copies.append(pltpu.make_async_copy(gram_v.at[top], gram_out.at[top], sem.at[2]))
    copies[-1].start()
    gram_v[bottom, top] = jnp.transpose(blocks[1])
    gram_v[bottom, bottom] = blocks[2]
    copies.append(pltpu.make_async_copy(gram_v.at[bottom], gram_out.at[bottom], sem.at[3]))
    copies[-1].start()
    for copy in copies:
        copy.wait()


def on_device(tile_values, tile_rows, tile_cols, tile_depths, tile_live, factor_b, factor_c, proj):
    n_ia, n_ja, n_ka = (lax.axis_size(name) for name in ("ia", "ja", "ka"))
    owners = n_ja * n_ka
    slot_total, tile = tile_values.shape
    slots = slot_total // owners
    rank = factor_b.shape[0]
    columns = proj.shape[1]
    half = columns // 2
    height = half // owners
    chunks_b, chunks_c = n_ia * n_ka, n_ia * n_ja
    vmem, dma = pltpu.VMEM, pltpu.SemaphoreType.DMA
    f32, bf16, i32 = jnp.float32, jnp.bfloat16, jnp.int32
    held = pl.pallas_call(
        functools.partial(kernel, n_ia, n_ja, n_ka),
        out_shape=(
            vmem((ROWS_DEV, columns), f32),
            vmem((rank, ROWS_DEV), f32),
            vmem((3, owners, height, half), bf16),
        ),
        in_specs=[pl.BlockSpec(memory_space=pl.ANY)] * 8,
        out_specs=tuple([pl.BlockSpec(memory_space=pltpu.VMEM)] * 3),
        scratch_shapes=[
            vmem((slot_total, tile), bf16),
            vmem((slot_total, tile), i32),
            vmem((slot_total, tile), i32),
            vmem((slot_total, tile), i32),
            vmem(proj.shape, f32),
            pltpu.SMEM((1, owners), i32),
            vmem((slot_total, tile), f32),
            vmem((chunks_b, rank, LANES), bf16),
            vmem((chunks_c, rank, LANES), bf16),
            vmem((chunks_b, rank, LANES), f32),
            vmem((chunks_c, rank, LANES), f32),
            vmem((owners, slots, tile), i32),
            vmem((owners, slots, tile), i32),
            vmem((owners, slots, 2 * rank, tile), bf16),
            vmem((owners, slots, 2 * rank, tile), bf16),
            vmem((columns, slots * tile), bf16),
            vmem((columns, ROWS_DEV), f32),
            vmem((columns, 4 * ROWS_DEV), bf16),
            vmem((columns, 4 * ROWS_DEV), bf16),
            vmem((3, owners, height, half), f32),
            vmem((3, owners, height, half), bf16),
            vmem((3, owners, height, half), bf16),
            vmem((3, height, half), bf16),
            vmem((3, n_ia, height, half), bf16),
            dma((8,)),
            dma((chunks_b,)), dma((chunks_b,)),
            dma((chunks_c,)), dma((chunks_c,)),
            dma((owners,)), dma((owners,)),
            dma((owners,)), dma((owners,)),
            dma((3, owners)), dma((3, owners)),
            dma((3, n_ia)), dma((3, n_ia)),
            dma((3, owners)), dma((3, owners)),
        ],
        compiler_params=pltpu.CompilerParams(collective_id=0, has_side_effects=True),
    )(
        tile_values, tile_rows, tile_cols, tile_depths, tile_live,
        factor_b[:, 0, :], factor_c[:, 0, :], proj,
    )
    return pl.pallas_call(
        finish,
        out_shape=(
            jax.ShapeDtypeStruct((ROWS_DEV, columns), f32),
            jax.ShapeDtypeStruct((columns, columns), f32),
            jax.ShapeDtypeStruct((rank, ROWS_DEV), f32),
        ),
        in_specs=[pl.BlockSpec(memory_space=pltpu.VMEM)] * 3,
        out_specs=tuple([pl.BlockSpec(memory_space=pl.ANY)] * 3),
        scratch_shapes=[vmem((columns, columns), f32), dma((4,))],
    )(*(pltpu.with_memory_space_constraint(array, vmem) for array in held))


def solution(mesh):
    return jax.shard_map(
        on_device,
        mesh=mesh,
        in_specs=(
            P(("ia", "ja", "ka"), None),
            P(("ia", "ja", "ka"), None),
            P(("ia", "ja", "ka"), None),
            P(("ia", "ja", "ka"), None),
            P(("ia", "ja", "ka"), None),
            P(None, "ja", ("ia", "ka")),
            P(None, "ka", ("ia", "ja")),
            P(),
        ),
        out_specs=(P(("ia", "ja", "ka"), None), P(), P(None, ("ia", "ja", "ka"))),
        check_vma=False,
    )
```

```python
import functools

import jax
import jax.numpy as jnp
from jax import lax
from jax.experimental import pallas as pl
from jax.experimental.pallas import tpu as pltpu
from jax.sharding import PartitionSpec as P

ROWS_DEV = 64
LANES = 128
MESH = pl.DeviceIdType.MESH


def each(begin, end):
    if end - begin > 16:
        return pl.loop(begin, end)

    def run(body):
        for step in range(begin, end):
            body(step)

    return run


def repeat(count, body, init):
    if count <= 16:
        for step in range(count):
            init = body(step, init)
        return init
    group = 8

    def turn(index, carry):
        for step in range(group):
            carry = body(index * group + step, carry)
        return carry

    return lax.fori_loop(0, count // group, turn, init)


def lookup(table, index):
    chunks, rank, _ = table.shape
    high = jnp.broadcast_to(lax.shift_right_logical(index, LANES.bit_length() - 1), (rank, LANES))
    low = jnp.broadcast_to(index & (LANES - 1), (rank, LANES))

    def step(chunk, found):
        here = jnp.take_along_axis(table[chunk], low, axis=1, mode="promise_in_bounds")
        return jnp.where(high == chunk, here, found)

    return repeat(chunks, step, jnp.zeros((rank, LANES), jnp.float32))


def kernel(
    n_ia, n_ja, n_ka,
    values, rows, cols, depths, live, fb, fc, proj,
    y_out, nf_out, final,
    values_v, rows_v, cols_v, depths_v, proj_v, live_s, scale_v,
    tb_in, tc_in, tb, tc,
    rows_send, rows_recv, pay_send, pay_recv, kron,
    yt_v, g_left, g_right, g_own, g_send, g_recv, z_send, z_recv,
    load_sem, tb_ssem, tb_rsem, tc_ssem, tc_rsem, rows_ssem, rows_rsem, pay_ssem, pay_rsem,
    g_ssem, g_rsem, z_ssem, z_rsem, f_ssem, f_rsem,
):
    owners = n_ja * n_ka
    slots = values.shape[0] // owners
    rank = fb.shape[0]
    a, b, c = lax.axis_index("ia"), lax.axis_index("ja"), lax.axis_index("ka")
    me_b = a * n_ka + c
    me_c = a * n_ja + b
    me_o = b * n_ka + c

    def b_peer(j):
        peer = lax.rem(me_b + j, n_ia * n_ka)
        return (peer // n_ka, b, lax.rem(peer, n_ka))

    def c_peer(j):
        peer = lax.rem(me_c + j, n_ia * n_ja)
        return (peer // n_ja, lax.rem(peer, n_ja), c)

    def o_peer(j):
        return (a, lax.rem(b + j // n_ka, n_ja), lax.rem(c + j % n_ka, n_ka))

    def to_o(j):
        return lax.rem(b + j // n_ka, n_ja) * n_ka + lax.rem(c + j % n_ka, n_ka)

    def from_o(j):
        return lax.rem(b + n_ja - j // n_ka, n_ja) * n_ka + lax.rem(c + n_ka - j % n_ka, n_ka)

    def a_peer(j):
        return (lax.rem(a + j, n_ia), b, c)

    barrier = pltpu.get_barrier_semaphore()
    for count, peer in ((n_ia * n_ka, b_peer), (n_ia * n_ja, c_peer), (owners, o_peer)):
        @each(1, count)
        def _(j, peer=peer):
            pl.semaphore_signal(barrier, inc=1, device_id=peer(j), device_id_type=MESH)

    loads = []
    for index, (src, dst) in enumerate((
        (values, values_v), (rows, rows_v), (cols, cols_v), (depths, depths_v),
        (proj, proj_v), (live, live_s), (fb, tb_in.at[me_b]), (fc, tc_in.at[me_c]),
    )):
        loads.append(pltpu.make_async_copy(src, dst, load_sem.at[index]))
        loads[-1].start()

    pl.semaphore_wait(barrier, n_ia * n_ka + n_ia * n_ja + owners - 3)

    def remote(src, dst, ssem, rsem, peer):
        return pltpu.make_async_remote_copy(
            src_ref=src, dst_ref=dst, send_sem=ssem, recv_sem=rsem,
            device_id=peer, device_id_type=MESH,
        )

    def tb_copy(j, slot):
        return remote(fb, tb_in.at[slot], tb_ssem.at[j], tb_rsem.at[slot], b_peer(j))

    def tc_copy(j, slot):
        return remote(fc, tc_in.at[slot], tc_ssem.at[j], tc_rsem.at[slot], c_peer(j))

    @each(1, n_ia * n_ka)
    def _(j):
        tb_copy(j, me_b).start()

    @each(1, n_ia * n_ja)
    def _(j):
        tc_copy(j, me_c).start()

    for load in loads:
        load.wait()

    @each(0, owners)
    def _(o):
        for t in range(slots):
            rows_send[o, pl.ds(t, 1), :] = rows_v[pl.ds(o * slots + t, 1), :]

    scale_v[...] = values_v[...].astype(jnp.float32)
    tb[me_b] = tb_in[me_b].astype(jnp.float32)
    tc[me_c] = tc_in[me_c].astype(jnp.float32)

    def rows_copy(j, slot):
        return remote(
            rows_send.at[to_o(j)], rows_recv.at[slot],
            rows_ssem.at[j], rows_rsem.at[slot], o_peer(j),
        )

    def pay_copy(j, slot):
        return remote(
            pay_send.at[to_o(j)], pay_recv.at[slot],
            pay_ssem.at[j], pay_rsem.at[slot], o_peer(j),
        )

    @each(1, owners)
    def _(j):
        rows_copy(j, me_o).start()

    @each(1, n_ia * n_ka)
    def _(j):
        slot = lax.rem(me_b + n_ia * n_ka - j, n_ia * n_ka)
        tb_copy(j, slot).wait_recv()
        tb[slot] = tb_in[slot].astype(jnp.float32)

    @each(1, n_ia * n_ja)
    def _(j):
        slot = lax.rem(me_c + n_ia * n_ja - j, n_ia * n_ja)
        tc_copy(j, slot).wait_recv()
        tc[slot] = tc_in[slot].astype(jnp.float32)

    def fill(o):
        count = live_s[0, o]
        for t in range(slots):
            row = pl.ds(o * slots + t, 1)
            value = jnp.where(count > t, scale_v[row, :], 0.0)
            pay_send[o, t, pl.ds(0, rank), :] = (lookup(tb, cols_v[row, :]) * value).astype(jnp.bfloat16)
            pay_send[o, t, pl.ds(rank, rank), :] = lookup(tc, depths_v[row, :]).astype(jnp.bfloat16)

    @pl.loop(1, owners)
    def _(j):
        fill(to_o(owners - j))
        pay_copy(owners - j, me_o).start()

    fill(me_o)

    def block(payload, target):
        hot = []
        for t in range(slots):
            part = payload[t].astype(jnp.float32)
            depth = part[rank:]
            for p in range(rank):
                kron[pl.ds(p * rank, rank), pl.ds(t * LANES, LANES)] = (
                    part[p:p + 1] * depth
                ).astype(jnp.bfloat16)
            spot = lax.broadcasted_iota(jnp.int32, (ROWS_DEV, LANES), 0)
            hot.append((target[pl.ds(t, 1), :] == spot).astype(jnp.float32).astype(jnp.bfloat16))
        return lax.dot_general(
            kron[...], jnp.concatenate(hot, axis=1), (((1,), (1,)), ((), ())),
            preferred_element_type=jnp.float32,
        )

    yt_v[...] = block(pay_send.at[me_o], rows_send.at[me_o])

    @each(1, n_ia * n_ka)
    def _(j):
        tb_copy(j, me_b).wait_send()

    @each(1, n_ia * n_ja)
    def _(j):
        tc_copy(j, me_c).wait_send()

    @each(1, owners)
    def _(j):
        rows_copy(j, me_o).wait_send()

    @pl.loop(1, owners)
    def _(j):
        slot = from_o(j)
        rows_copy(j, slot).wait_recv()
        pay_copy(j, slot).wait_recv()
        yt_v[...] += block(pay_recv.at[slot], rows_recv.at[slot])

    def g_copy(j, slot):
        return remote(
            g_send.at[:, to_o(j)], g_recv.at[:, slot], g_ssem.at[j], g_rsem.at[slot], o_peer(j)
        )

    def z_copy(j, slot):
        return remote(z_send, z_recv.at[slot], z_ssem.at[j], z_rsem.at[slot], a_peer(j))

    def f_copy(j, slot):
        return remote(
            final.at[:, slot], final.at[:, slot], f_ssem.at[j], f_rsem.at[slot], o_peer(j)
        )

    half = kron.shape[0] // 2
    pieces = ((0, 0), (0, 1), (1, 1))
    yt = yt_v[...]
    high = yt.astype(jnp.bfloat16).astype(jnp.float32)
    low = yt - high
    g_left[...] = jnp.concatenate([high, low, high, low], axis=1).astype(jnp.bfloat16)
    g_right[...] = jnp.concatenate([high, high, low, low], axis=1).astype(jnp.bfloat16)
    scale = 1.0 / (ROWS_DEV * owners * n_ia)
    for i, (left, right) in enumerate(pieces):
        piece = lax.dot_general(
            g_left[pl.ds(left * half, half), :], g_right[pl.ds(right * half, half), :],
            (((1,), (1,)), ((), ())), preferred_element_type=jnp.float32,
        ) * scale
        g_own[i] = piece.reshape(g_own.shape[1:])
        g_send[i] = piece.reshape(g_own.shape[1:]).astype(jnp.bfloat16)

    @each(1, owners)
    def _(j):
        g_copy(owners - j, me_o).start()

    nf_out[...] = lax.dot_general(
        proj_v[...], yt_v[...], (((1,), (0,)), ((), ())),
        precision=lax.Precision.HIGHEST, preferred_element_type=jnp.float32,
    )
    y_out[...] = jnp.transpose(yt_v[...])

    @each(1, owners)
    def _(j):
        pay_copy(j, me_o).wait_send()

    total = g_own[:, me_o]
    for j in range(1, owners):
        slot = from_o(j)
        g_copy(j, slot).wait_recv()
        total = total + g_recv[:, slot].astype(jnp.float32)
    z_send[...] = total.astype(jnp.bfloat16)
    for j in range(1, n_ia):
        z_copy(j, a).start()
    z_recv[a] = total.astype(jnp.bfloat16)

    for j in range(1, n_ia):
        z_copy(j, lax.rem(a + n_ia - j, n_ia)).wait_recv()
    total = z_recv[0].astype(jnp.float32)
    for index in range(1, n_ia):
        total = total + z_recv[index].astype(jnp.float32)
    final[:, me_o] = total.astype(jnp.bfloat16)

    @each(1, owners)
    def _(j):
        f_copy(owners - j, me_o).start()

    @each(1, owners)
    def _(j):
        g_copy(j, me_o).wait_send()

    for j in range(1, n_ia):
        z_copy(j, a).wait_send()

    @each(1, owners)
    def _(j):
        f_copy(j, from_o(j)).wait_recv()

    @each(1, owners)
    def _(j):
        f_copy(j, me_o).wait_send()


def finish(y, nf, final, y_out, gram_out, nf_out, gram_v, sem):
    copies = [
        pltpu.make_async_copy(y, y_out, sem.at[0]),
        pltpu.make_async_copy(nf, nf_out, sem.at[1]),
    ]
    for copy in copies:
        copy.start()
    half = gram_v.shape[1] // 2
    blocks = [final[i].astype(jnp.float32).reshape(half, half) for i in range(3)]
    top, bottom = pl.ds(0, half), pl.ds(half, half)
    gram_v[top, top] = blocks[0]
    gram_v[top, bottom] = blocks[1]
    copies.append(pltpu.make_async_copy(gram_v.at[top], gram_out.at[top], sem.at[2]))
    copies[-1].start()
    gram_v[bottom, top] = jnp.transpose(blocks[1])
    gram_v[bottom, bottom] = blocks[2]
    copies.append(pltpu.make_async_copy(gram_v.at[bottom], gram_out.at[bottom], sem.at[3]))
    copies[-1].start()
    for copy in copies:
        copy.wait()


def on_device(tile_values, tile_rows, tile_cols, tile_depths, tile_live, factor_b, factor_c, proj):
    n_ia, n_ja, n_ka = (lax.axis_size(name) for name in ("ia", "ja", "ka"))
    owners = n_ja * n_ka
    slot_total, tile = tile_values.shape
    slots = slot_total // owners
    rank = factor_b.shape[0]
    columns = proj.shape[1]
    half = columns // 2
    height = half // owners
    chunks_b, chunks_c = n_ia * n_ka, n_ia * n_ja
    vmem, dma = pltpu.VMEM, pltpu.SemaphoreType.DMA
    f32, bf16, i32 = jnp.float32, jnp.bfloat16, jnp.int32
    held = pl.pallas_call(
        functools.partial(kernel, n_ia, n_ja, n_ka),
        out_shape=(
            vmem((ROWS_DEV, columns), f32),
            vmem((rank, ROWS_DEV), f32),
            vmem((3, owners, height, half), bf16),
        ),
        in_specs=[pl.BlockSpec(memory_space=pl.ANY)] * 8,
        out_specs=tuple([pl.BlockSpec(memory_space=pltpu.VMEM)] * 3),
        scratch_shapes=[
            vmem((slot_total, tile), bf16),
            vmem((slot_total, tile), i32),
            vmem((slot_total, tile), i32),
            vmem((slot_total, tile), i32),
            vmem(proj.shape, f32),
            pltpu.SMEM((1, owners), i32),
            vmem((slot_total, tile), f32),
            vmem((chunks_b, rank, LANES), bf16),
            vmem((chunks_c, rank, LANES), bf16),
            vmem((chunks_b, rank, LANES), f32),
            vmem((chunks_c, rank, LANES), f32),
            vmem((owners, slots, tile), i32),
            vmem((owners, slots, tile), i32),
            vmem((owners, slots, 2 * rank, tile), bf16),
            vmem((owners, slots, 2 * rank, tile), bf16),
            vmem((columns, slots * tile), bf16),
            vmem((columns, ROWS_DEV), f32),
            vmem((columns, 4 * ROWS_DEV), bf16),
            vmem((columns, 4 * ROWS_DEV), bf16),
            vmem((3, owners, height, half), f32),
            vmem((3, owners, height, half), bf16),
            vmem((3, owners, height, half), bf16),
            vmem((3, height, half), bf16),
            vmem((n_ia, 3, height, half), bf16),
            dma((8,)),
            dma((chunks_b,)), dma((chunks_b,)),
            dma((chunks_c,)), dma((chunks_c,)),
            dma((owners,)), dma((owners,)),
            dma((owners,)), dma((owners,)),
            dma((owners,)), dma((owners,)),
            dma((n_ia,)), dma((n_ia,)),
            dma((owners,)), dma((owners,)),
        ],
        compiler_params=pltpu.CompilerParams(collective_id=0, has_side_effects=True),
    )(
        tile_values, tile_rows, tile_cols, tile_depths, tile_live,
        factor_b[:, 0, :], factor_c[:, 0, :], proj,
    )
    return pl.pallas_call(
        finish,
        out_shape=(
            jax.ShapeDtypeStruct((ROWS_DEV, columns), f32),
            jax.ShapeDtypeStruct((columns, columns), f32),
            jax.ShapeDtypeStruct((rank, ROWS_DEV), f32),
        ),
        in_specs=[pl.BlockSpec(memory_space=pltpu.VMEM)] * 3,
        out_specs=tuple([pl.BlockSpec(memory_space=pl.ANY)] * 3),
        scratch_shapes=[vmem((columns, columns), f32), dma((4,))],
    )(*(pltpu.with_memory_space_constraint(array, vmem) for array in held))


def solution(mesh):
    return jax.shard_map(
        on_device,
        mesh=mesh,
        in_specs=(
            P(("ia", "ja", "ka"), None),
            P(("ia", "ja", "ka"), None),
            P(("ia", "ja", "ka"), None),
            P(("ia", "ja", "ka"), None),
            P(("ia", "ja", "ka"), None),
            P(None, "ja", ("ia", "ka")),
            P(None, "ka", ("ia", "ja")),
            P(),
        ),
        out_specs=(P(("ia", "ja", "ka"), None), P(), P(None, ("ia", "ja", "ka"))),
        check_vma=False,
    )
```

```python
import functools

import jax
import jax.numpy as jnp
from jax import lax
from jax.experimental import pallas as pl
from jax.experimental.pallas import tpu as pltpu
from jax.sharding import PartitionSpec as P

ROWS_DEV = 64
LANES = 128
MESH = pl.DeviceIdType.MESH


def each(begin, end):
    if end - begin > 16:
        return pl.loop(begin, end)

    def run(body):
        for step in range(begin, end):
            body(step)

    return run


def repeat(count, body, init):
    if count <= 16:
        for step in range(count):
            init = body(step, init)
        return init
    group = 8

    def turn(index, carry):
        for step in range(group):
            carry = body(index * group + step, carry)
        return carry

    return lax.fori_loop(0, count // group, turn, init)


def lookup(table, index):
    chunks, rank, _ = table.shape
    high = jnp.broadcast_to(lax.shift_right_logical(index, LANES.bit_length() - 1), (rank, LANES))
    low = jnp.broadcast_to(index & (LANES - 1), (rank, LANES))

    def step(chunk, found):
        here = jnp.take_along_axis(table[chunk], low, axis=1, mode="promise_in_bounds")
        return jnp.where(high == chunk, here, found)

    return repeat(chunks, step, jnp.zeros((rank, LANES), jnp.float32))


def kernel(
    n_ia, n_ja, n_ka,
    values, rows, cols, depths, live, fb, fc, proj,
    y_out, nf_out, final,
    values_v, rows_v, cols_v, depths_v, proj_v, live_s, scale_v,
    tb_in, tc_in, tb, tc,
    rows_send, rows_recv, pay_send, pay_recv, kron,
    yt_v, g_left, g_right, g_own, g_send, g_recv, z_send, z_recv,
    load_sem, tb_ssem, tb_rsem, tc_ssem, tc_rsem, rows_ssem, rows_rsem, pay_ssem, pay_rsem,
    g_ssem, g_rsem, z_ssem, z_rsem, f_ssem, f_rsem,
):
    owners = n_ja * n_ka
    slots = values.shape[0] // owners
    rank = fb.shape[0]
    a, b, c = lax.axis_index("ia"), lax.axis_index("ja"), lax.axis_index("ka")
    me_b = a * n_ka + c
    me_c = a * n_ja + b
    me_o = b * n_ka + c

    def b_peer(j):
        peer = lax.rem(me_b + j, n_ia * n_ka)
        return (peer // n_ka, b, lax.rem(peer, n_ka))

    def c_peer(j):
        peer = lax.rem(me_c + j, n_ia * n_ja)
        return (peer // n_ja, lax.rem(peer, n_ja), c)

    def o_peer(j):
        return (a, lax.rem(b + j // n_ka, n_ja), lax.rem(c + j % n_ka, n_ka))

    def to_o(j):
        return lax.rem(b + j // n_ka, n_ja) * n_ka + lax.rem(c + j % n_ka, n_ka)

    def from_o(j):
        return lax.rem(b + n_ja - j // n_ka, n_ja) * n_ka + lax.rem(c + n_ka - j % n_ka, n_ka)

    def a_peer(j):
        return (lax.rem(a + j, n_ia), b, c)

    barrier = pltpu.get_barrier_semaphore()
    for count, peer in ((n_ia * n_ka, b_peer), (n_ia * n_ja, c_peer), (owners, o_peer)):
        @each(1, count)
        def _(j, peer=peer):
            pl.semaphore_signal(barrier, inc=1, device_id=peer(j), device_id_type=MESH)

    loads = []
    for index, (src, dst) in enumerate((
        (values, values_v), (rows, rows_v), (cols, cols_v), (depths, depths_v),
        (proj, proj_v), (live, live_s), (fb, tb_in.at[me_b]), (fc, tc_in.at[me_c]),
    )):
        loads.append(pltpu.make_async_copy(src, dst, load_sem.at[index]))
        loads[-1].start()

    pl.semaphore_wait(barrier, n_ia * n_ka + n_ia * n_ja + owners - 3)

    def remote(src, dst, ssem, rsem, peer):
        return pltpu.make_async_remote_copy(
            src_ref=src, dst_ref=dst, send_sem=ssem, recv_sem=rsem,
            device_id=peer, device_id_type=MESH,
        )

    def tb_copy(j, slot):
        return remote(fb, tb_in.at[slot], tb_ssem.at[j], tb_rsem.at[slot], b_peer(j))

    def tc_copy(j, slot):
        return remote(fc, tc_in.at[slot], tc_ssem.at[j], tc_rsem.at[slot], c_peer(j))

    @each(1, n_ia * n_ja)
    def _(j):
        tc_copy(n_ia * n_ja - j, me_c).start()

    @each(1, n_ia * n_ka)
    def _(j):
        tb_copy(n_ia * n_ka - j, me_b).start()

    for load in loads:
        load.wait()

    @each(0, owners)
    def _(o):
        for t in range(slots):
            rows_send[o, pl.ds(t, 1), :] = rows_v[pl.ds(o * slots + t, 1), :]

    scale_v[...] = values_v[...].astype(jnp.float32)
    tb[me_b] = tb_in[me_b].astype(jnp.float32)
    tc[me_c] = tc_in[me_c].astype(jnp.float32)

    def rows_copy(j, slot):
        return remote(
            rows_send.at[to_o(j)], rows_recv.at[slot],
            rows_ssem.at[j], rows_rsem.at[slot], o_peer(j),
        )

    def pay_copy(j, slot):
        return remote(
            pay_send.at[to_o(j)], pay_recv.at[slot],
            pay_ssem.at[j], pay_rsem.at[slot], o_peer(j),
        )

    @each(1, owners)
    def _(j):
        rows_copy(j, me_o).start()

    @each(1, n_ia * n_ka)
    def _(j):
        slot = lax.rem(me_b + n_ia * n_ka - j, n_ia * n_ka)
        tb_copy(j, slot).wait_recv()
        tb[slot] = tb_in[slot].astype(jnp.float32)

    @each(1, n_ia * n_ja)
    def _(j):
        slot = lax.rem(me_c + n_ia * n_ja - j, n_ia * n_ja)
        tc_copy(j, slot).wait_recv()
        tc[slot] = tc_in[slot].astype(jnp.float32)

    def fill(o):
        count = live_s[0, o]
        for t in range(slots):
            row = pl.ds(o * slots + t, 1)
            value = jnp.where(count > t, scale_v[row, :], 0.0)
            pay_send[o, t, pl.ds(0, rank), :] = (lookup(tb, cols_v[row, :]) * value).astype(jnp.bfloat16)
            pay_send[o, t, pl.ds(rank, rank), :] = lookup(tc, depths_v[row, :]).astype(jnp.bfloat16)

    @pl.loop(1, owners)
    def _(j):
        fill(to_o(owners - j))
        pay_copy(owners - j, me_o).start()

    fill(me_o)

    def block(payload, target):
        hot = []
        for t in range(slots):
            part = payload[t].astype(jnp.float32)
            depth = part[rank:]
            for p in range(rank):
                kron[pl.ds(p * rank, rank), pl.ds(t * LANES, LANES)] = (
                    part[p:p + 1] * depth
                ).astype(jnp.bfloat16)
            spot = lax.broadcasted_iota(jnp.int32, (ROWS_DEV, LANES), 0)
            hot.append((target[pl.ds(t, 1), :] == spot).astype(jnp.float32).astype(jnp.bfloat16))
        return lax.dot_general(
            kron[...], jnp.concatenate(hot, axis=1), (((1,), (1,)), ((), ())),
            preferred_element_type=jnp.float32,
        )

    yt_v[...] = block(pay_send.at[me_o], rows_send.at[me_o])

    @each(1, n_ia * n_ka)
    def _(j):
        tb_copy(j, me_b).wait_send()

    @each(1, n_ia * n_ja)
    def _(j):
        tc_copy(j, me_c).wait_send()

    @each(1, owners)
    def _(j):
        rows_copy(j, me_o).wait_send()

    @pl.loop(1, owners)
    def _(j):
        slot = from_o(j)
        rows_copy(j, slot).wait_recv()
        pay_copy(j, slot).wait_recv()
        yt_v[...] += block(pay_recv.at[slot], rows_recv.at[slot])

    def g_copy(j, slot):
        return remote(
            g_send.at[:, to_o(j)], g_recv.at[:, slot], g_ssem.at[j], g_rsem.at[slot], o_peer(j)
        )

    def z_copy(j, slot):
        return remote(z_send, z_recv.at[slot], z_ssem.at[j], z_rsem.at[slot], a_peer(j))

    def f_copy(j, slot):
        return remote(
            final.at[:, slot], final.at[:, slot], f_ssem.at[j], f_rsem.at[slot], o_peer(j)
        )

    half = kron.shape[0] // 2
    pieces = ((0, 0), (0, 1), (1, 1))
    yt = yt_v[...]
    high = yt.astype(jnp.bfloat16).astype(jnp.float32)
    low = yt - high
    g_left[...] = jnp.concatenate([high, low, high, low], axis=1).astype(jnp.bfloat16)
    g_right[...] = jnp.concatenate([high, high, low, low], axis=1).astype(jnp.bfloat16)
    scale = 1.0 / (ROWS_DEV * owners * n_ia)
    for i, (left, right) in enumerate(pieces):
        piece = lax.dot_general(
            g_left[pl.ds(left * half, half), :], g_right[pl.ds(right * half, half), :],
            (((1,), (1,)), ((), ())), preferred_element_type=jnp.float32,
        ) * scale
        g_own[i] = piece.reshape(g_own.shape[1:])
        g_send[i] = piece.reshape(g_own.shape[1:]).astype(jnp.bfloat16)

    @each(1, owners)
    def _(j):
        g_copy(owners - j, me_o).start()

    nf_out[...] = lax.dot_general(
        proj_v[...], yt_v[...], (((1,), (0,)), ((), ())),
        precision=lax.Precision.HIGHEST, preferred_element_type=jnp.float32,
    )
    y_out[...] = jnp.transpose(yt_v[...])

    @each(1, owners)
    def _(j):
        pay_copy(j, me_o).wait_send()

    total = g_own[:, me_o]
    for j in range(1, owners):
        slot = from_o(j)
        g_copy(j, slot).wait_recv()
        total = total + g_recv[:, slot].astype(jnp.float32)
    z_send[...] = total.astype(jnp.bfloat16)
    for j in range(1, n_ia):
        z_copy(j, a).start()
    z_recv[a] = total.astype(jnp.bfloat16)

    for j in range(1, n_ia):
        z_copy(j, lax.rem(a + n_ia - j, n_ia)).wait_recv()
    total = z_recv[0].astype(jnp.float32)
    for index in range(1, n_ia):
        total = total + z_recv[index].astype(jnp.float32)
    final[:, me_o] = total.astype(jnp.bfloat16)

    @each(1, owners)
    def _(j):
        f_copy(owners - j, me_o).start()

    @each(1, owners)
    def _(j):
        g_copy(j, me_o).wait_send()

    for j in range(1, n_ia):
        z_copy(j, a).wait_send()

    @each(1, owners)
    def _(j):
        f_copy(j, from_o(j)).wait_recv()

    @each(1, owners)
    def _(j):
        f_copy(j, me_o).wait_send()


def finish(y, nf, final, y_out, gram_out, nf_out, gram_v, sem):
    copies = [
        pltpu.make_async_copy(y, y_out, sem.at[0]),
        pltpu.make_async_copy(nf, nf_out, sem.at[1]),
    ]
    for copy in copies:
        copy.start()
    half = gram_v.shape[1] // 2
    blocks = [final[i].astype(jnp.float32).reshape(half, half) for i in range(3)]
    top, bottom = pl.ds(0, half), pl.ds(half, half)
    gram_v[top, top] = blocks[0]
    gram_v[top, bottom] = blocks[1]
    copies.append(pltpu.make_async_copy(gram_v.at[top], gram_out.at[top], sem.at[2]))
    copies[-1].start()
    gram_v[bottom, top] = jnp.transpose(blocks[1])
    gram_v[bottom, bottom] = blocks[2]
    copies.append(pltpu.make_async_copy(gram_v.at[bottom], gram_out.at[bottom], sem.at[3]))
    copies[-1].start()
    for copy in copies:
        copy.wait()


def on_device(tile_values, tile_rows, tile_cols, tile_depths, tile_live, factor_b, factor_c, proj):
    n_ia, n_ja, n_ka = (lax.axis_size(name) for name in ("ia", "ja", "ka"))
    owners = n_ja * n_ka
    slot_total, tile = tile_values.shape
    slots = slot_total // owners
    rank = factor_b.shape[0]
    columns = proj.shape[1]
    half = columns // 2
    height = half // owners
    chunks_b, chunks_c = n_ia * n_ka, n_ia * n_ja
    vmem, dma = pltpu.VMEM, pltpu.SemaphoreType.DMA
    f32, bf16, i32 = jnp.float32, jnp.bfloat16, jnp.int32
    held = pl.pallas_call(
        functools.partial(kernel, n_ia, n_ja, n_ka),
        out_shape=(
            vmem((ROWS_DEV, columns), f32),
            vmem((rank, ROWS_DEV), f32),
            vmem((3, owners, height, half), bf16),
        ),
        in_specs=[pl.BlockSpec(memory_space=pl.ANY)] * 8,
        out_specs=tuple([pl.BlockSpec(memory_space=pltpu.VMEM)] * 3),
        scratch_shapes=[
            vmem((slot_total, tile), bf16),
            vmem((slot_total, tile), i32),
            vmem((slot_total, tile), i32),
            vmem((slot_total, tile), i32),
            vmem(proj.shape, f32),
            pltpu.SMEM((1, owners), i32),
            vmem((slot_total, tile), f32),
            vmem((chunks_b, rank, LANES), bf16),
            vmem((chunks_c, rank, LANES), bf16),
            vmem((chunks_b, rank, LANES), f32),
            vmem((chunks_c, rank, LANES), f32),
            vmem((owners, slots, tile), i32),
            vmem((owners, slots, tile), i32),
            vmem((owners, slots, 2 * rank, tile), bf16),
            vmem((owners, slots, 2 * rank, tile), bf16),
            vmem((columns, slots * tile), bf16),
            vmem((columns, ROWS_DEV), f32),
            vmem((columns, 4 * ROWS_DEV), bf16),
            vmem((columns, 4 * ROWS_DEV), bf16),
            vmem((3, owners, height, half), f32),
            vmem((3, owners, height, half), bf16),
            vmem((3, owners, height, half), bf16),
            vmem((3, height, half), bf16),
            vmem((n_ia, 3, height, half), bf16),
            dma((8,)),
            dma((chunks_b,)), dma((chunks_b,)),
            dma((chunks_c,)), dma((chunks_c,)),
            dma((owners,)), dma((owners,)),
            dma((owners,)), dma((owners,)),
            dma((owners,)), dma((owners,)),
            dma((n_ia,)), dma((n_ia,)),
            dma((owners,)), dma((owners,)),
        ],
        compiler_params=pltpu.CompilerParams(collective_id=0, has_side_effects=True),
    )(
        tile_values, tile_rows, tile_cols, tile_depths, tile_live,
        factor_b[:, 0, :], factor_c[:, 0, :], proj,
    )
    return pl.pallas_call(
        finish,
        out_shape=(
            jax.ShapeDtypeStruct((ROWS_DEV, columns), f32),
            jax.ShapeDtypeStruct((columns, columns), f32),
            jax.ShapeDtypeStruct((rank, ROWS_DEV), f32),
        ),
        in_specs=[pl.BlockSpec(memory_space=pltpu.VMEM)] * 3,
        out_specs=tuple([pl.BlockSpec(memory_space=pl.ANY)] * 3),
        scratch_shapes=[vmem((columns, columns), f32), dma((4,))],
    )(*(pltpu.with_memory_space_constraint(array, vmem) for array in held))


def solution(mesh):
    return jax.shard_map(
        on_device,
        mesh=mesh,
        in_specs=(
            P(("ia", "ja", "ka"), None),
            P(("ia", "ja", "ka"), None),
            P(("ia", "ja", "ka"), None),
            P(("ia", "ja", "ka"), None),
            P(("ia", "ja", "ka"), None),
            P(None, "ja", ("ia", "ka")),
            P(None, "ka", ("ia", "ja")),
            P(),
        ),
        out_specs=(P(("ia", "ja", "ka"), None), P(), P(None, ("ia", "ja", "ka"))),
        check_vma=False,
    )
```

```python
import functools

import jax
import jax.numpy as jnp
from jax import lax
from jax.experimental import pallas as pl
from jax.experimental.pallas import tpu as pltpu
from jax.sharding import PartitionSpec as P

ROWS_DEV = 64
LANES = 128
MESH = pl.DeviceIdType.MESH


def each(begin, end):
    if end - begin > 16:
        return pl.loop(begin, end)

    def run(body):
        for step in range(begin, end):
            body(step)

    return run


def repeat(count, body, init):
    if count <= 16:
        for step in range(count):
            init = body(step, init)
        return init
    group = 8

    def turn(index, carry):
        for step in range(group):
            carry = body(index * group + step, carry)
        return carry

    return lax.fori_loop(0, count // group, turn, init)


def lookup(table, index):
    chunks, rank, _ = table.shape
    high = jnp.broadcast_to(lax.shift_right_logical(index, LANES.bit_length() - 1), (rank, LANES))
    low = jnp.broadcast_to(index & (LANES - 1), (rank, LANES))

    def step(chunk, found):
        here = jnp.take_along_axis(table[chunk], low, axis=1, mode="promise_in_bounds")
        return jnp.where(high == chunk, here, found)

    return repeat(chunks, step, jnp.zeros((rank, LANES), jnp.float32))


def kernel(
    n_ia, n_ja, n_ka,
    values, rows, cols, depths, live, fb, fc, proj,
    y_out, nf_out, final,
    values_v, rows_v, cols_v, depths_v, proj_v, live_s, scale_v,
    tb_in, tc_in, tb, tc,
    rows_send, rows_recv, pay_send, pay_recv, kron,
    yt_v, g_left, g_right, g_own, g_send, g_recv, z_send, z_recv,
    load_sem, tb_ssem, tb_rsem, tc_ssem, tc_rsem, rows_ssem, rows_rsem, pay_ssem, pay_rsem,
    g_ssem, g_rsem, z_ssem, z_rsem, f_ssem, f_rsem,
):
    owners = n_ja * n_ka
    slots = values.shape[0] // owners
    rank = fb.shape[0]
    a, b, c = lax.axis_index("ia"), lax.axis_index("ja"), lax.axis_index("ka")
    me_b = a * n_ka + c
    me_c = a * n_ja + b
    me_o = b * n_ka + c

    def b_peer(j):
        peer = lax.rem(me_b + j, n_ia * n_ka)
        return (peer // n_ka, b, lax.rem(peer, n_ka))

    def c_peer(j):
        peer = lax.rem(me_c + j, n_ia * n_ja)
        return (peer // n_ja, lax.rem(peer, n_ja), c)

    def o_peer(j):
        return (a, lax.rem(b + j // n_ka, n_ja), lax.rem(c + j % n_ka, n_ka))

    def to_o(j):
        return lax.rem(b + j // n_ka, n_ja) * n_ka + lax.rem(c + j % n_ka, n_ka)

    def from_o(j):
        return lax.rem(b + n_ja - j // n_ka, n_ja) * n_ka + lax.rem(c + n_ka - j % n_ka, n_ka)

    def a_peer(j):
        return (lax.rem(a + j, n_ia), b, c)

    barrier = pltpu.get_barrier_semaphore()
    for count, peer in ((n_ia * n_ka, b_peer), (n_ia * n_ja, c_peer), (owners, o_peer)):
        @each(1, count)
        def _(j, peer=peer, count=count):
            pl.semaphore_signal(barrier, inc=1, device_id=peer(count - j), device_id_type=MESH)

    loads = []
    for index, (src, dst) in enumerate((
        (values, values_v), (rows, rows_v), (cols, cols_v), (depths, depths_v),
        (proj, proj_v), (live, live_s), (fb, tb_in.at[me_b]), (fc, tc_in.at[me_c]),
    )):
        loads.append(pltpu.make_async_copy(src, dst, load_sem.at[index]))
        loads[-1].start()

    pl.semaphore_wait(barrier, n_ia * n_ka + n_ia * n_ja + owners - 3)

    def remote(src, dst, ssem, rsem, peer):
        return pltpu.make_async_remote_copy(
            src_ref=src, dst_ref=dst, send_sem=ssem, recv_sem=rsem,
            device_id=peer, device_id_type=MESH,
        )

    def tb_copy(j, slot):
        return remote(fb, tb_in.at[slot], tb_ssem.at[j], tb_rsem.at[slot], b_peer(j))

    def tc_copy(j, slot):
        return remote(fc, tc_in.at[slot], tc_ssem.at[j], tc_rsem.at[slot], c_peer(j))

    @each(1, n_ia * n_ja)
    def _(j):
        tc_copy(n_ia * n_ja - j, me_c).start()

    @each(1, n_ia * n_ka)
    def _(j):
        tb_copy(n_ia * n_ka - j, me_b).start()

    for load in loads:
        load.wait()

    @each(0, owners)
    def _(o):
        for t in range(slots):
            rows_send[o, pl.ds(t, 1), :] = rows_v[pl.ds(o * slots + t, 1), :]

    scale_v[...] = values_v[...].astype(jnp.float32)
    tb[me_b] = tb_in[me_b].astype(jnp.float32)
    tc[me_c] = tc_in[me_c].astype(jnp.float32)

    def rows_copy(j, slot):
        return remote(
            rows_send.at[to_o(j)], rows_recv.at[slot],
            rows_ssem.at[j], rows_rsem.at[slot], o_peer(j),
        )

    def pay_copy(j, slot):
        return remote(
            pay_send.at[to_o(j)], pay_recv.at[slot],
            pay_ssem.at[j], pay_rsem.at[slot], o_peer(j),
        )

    @each(1, owners)
    def _(j):
        rows_copy(j, me_o).start()

    @each(1, n_ia * n_ka)
    def _(j):
        slot = lax.rem(me_b + n_ia * n_ka - j, n_ia * n_ka)
        tb_copy(j, slot).wait_recv()
        tb[slot] = tb_in[slot].astype(jnp.float32)

    @each(1, n_ia * n_ja)
    def _(j):
        slot = lax.rem(me_c + n_ia * n_ja - j, n_ia * n_ja)
        tc_copy(j, slot).wait_recv()
        tc[slot] = tc_in[slot].astype(jnp.float32)

    def fill(o):
        count = live_s[0, o]
        for t in range(slots):
            row = pl.ds(o * slots + t, 1)
            value = jnp.where(count > t, scale_v[row, :], 0.0)
            pay_send[o, t, pl.ds(0, rank), :] = (lookup(tb, cols_v[row, :]) * value).astype(jnp.bfloat16)
            pay_send[o, t, pl.ds(rank, rank), :] = lookup(tc, depths_v[row, :]).astype(jnp.bfloat16)

    @pl.loop(1, owners)
    def _(j):
        fill(to_o(owners - j))
        pay_copy(owners - j, me_o).start()

    fill(me_o)

    def block(payload, target):
        hot = []
        for t in range(slots):
            part = payload[t].astype(jnp.float32)
            depth = part[rank:]
            for p in range(rank):
                kron[pl.ds(p * rank, rank), pl.ds(t * LANES, LANES)] = (
                    part[p:p + 1] * depth
                ).astype(jnp.bfloat16)
            spot = lax.broadcasted_iota(jnp.int32, (ROWS_DEV, LANES), 0)
            hot.append((target[pl.ds(t, 1), :] == spot).astype(jnp.float32).astype(jnp.bfloat16))
        return lax.dot_general(
            kron[...], jnp.concatenate(hot, axis=1), (((1,), (1,)), ((), ())),
            preferred_element_type=jnp.float32,
        )

    yt_v[...] = block(pay_send.at[me_o], rows_send.at[me_o])

    @each(1, n_ia * n_ka)
    def _(j):
        tb_copy(j, me_b).wait_send()

    @each(1, n_ia * n_ja)
    def _(j):
        tc_copy(j, me_c).wait_send()

    @each(1, owners)
    def _(j):
        rows_copy(j, me_o).wait_send()

    @pl.loop(1, owners)
    def _(j):
        slot = from_o(j)
        rows_copy(j, slot).wait_recv()
        pay_copy(j, slot).wait_recv()
        yt_v[...] += block(pay_recv.at[slot], rows_recv.at[slot])

    def g_copy(j, slot):
        return remote(
            g_send.at[:, to_o(j)], g_recv.at[:, slot], g_ssem.at[j], g_rsem.at[slot], o_peer(j)
        )

    def z_copy(j, slot):
        return remote(z_send, z_recv.at[slot], z_ssem.at[j], z_rsem.at[slot], a_peer(j))

    def f_copy(j, slot):
        return remote(
            final.at[:, slot], final.at[:, slot], f_ssem.at[j], f_rsem.at[slot], o_peer(j)
        )

    half = kron.shape[0] // 2
    pieces = ((0, 0), (0, 1), (1, 1))
    yt = yt_v[...]
    high = yt.astype(jnp.bfloat16).astype(jnp.float32)
    low = yt - high
    g_left[...] = jnp.concatenate([high, low, high, low], axis=1).astype(jnp.bfloat16)
    g_right[...] = jnp.concatenate([high, high, low, low], axis=1).astype(jnp.bfloat16)
    scale = 1.0 / (ROWS_DEV * owners * n_ia)
    for i, (left, right) in enumerate(pieces):
        piece = lax.dot_general(
            g_left[pl.ds(left * half, half), :], g_right[pl.ds(right * half, half), :],
            (((1,), (1,)), ((), ())), preferred_element_type=jnp.float32,
        ) * scale
        g_own[i] = piece.reshape(g_own.shape[1:])
        g_send[i] = piece.reshape(g_own.shape[1:]).astype(jnp.bfloat16)

    @each(1, owners)
    def _(j):
        g_copy(owners - j, me_o).start()

    nf_out[...] = lax.dot_general(
        proj_v[...], yt_v[...], (((1,), (0,)), ((), ())),
        precision=lax.Precision.HIGHEST, preferred_element_type=jnp.float32,
    )
    y_out[...] = jnp.transpose(yt_v[...])

    @each(1, owners)
    def _(j):
        pay_copy(j, me_o).wait_send()

    total = g_own[:, me_o]
    for j in range(1, owners):
        slot = from_o(j)
        g_copy(j, slot).wait_recv()
        total = total + g_recv[:, slot].astype(jnp.float32)
    z_send[...] = total.astype(jnp.bfloat16)
    for j in range(n_ia - 1, 0, -1):
        z_copy(j, a).start()
    z_recv[a] = total.astype(jnp.bfloat16)

    for j in range(1, n_ia):
        z_copy(j, lax.rem(a + n_ia - j, n_ia)).wait_recv()
    total = z_recv[0].astype(jnp.float32)
    for index in range(1, n_ia):
        total = total + z_recv[index].astype(jnp.float32)
    final[:, me_o] = total.astype(jnp.bfloat16)

    @each(1, owners)
    def _(j):
        f_copy(owners - j, me_o).start()

    @each(1, owners)
    def _(j):
        g_copy(j, me_o).wait_send()

    for j in range(1, n_ia):
        z_copy(j, a).wait_send()

    @each(1, owners)
    def _(j):
        f_copy(j, from_o(j)).wait_recv()

    @each(1, owners)
    def _(j):
        f_copy(j, me_o).wait_send()


def finish(y, nf, final, y_out, gram_out, nf_out, gram_v, sem):
    copies = [
        pltpu.make_async_copy(y, y_out, sem.at[0]),
        pltpu.make_async_copy(nf, nf_out, sem.at[1]),
    ]
    for copy in copies:
        copy.start()
    half = gram_v.shape[1] // 2
    blocks = [final[i].astype(jnp.float32).reshape(half, half) for i in range(3)]
    top, bottom = pl.ds(0, half), pl.ds(half, half)
    gram_v[top, top] = blocks[0]
    gram_v[top, bottom] = blocks[1]
    copies.append(pltpu.make_async_copy(gram_v.at[top], gram_out.at[top], sem.at[2]))
    copies[-1].start()
    gram_v[bottom, top] = jnp.transpose(blocks[1])
    gram_v[bottom, bottom] = blocks[2]
    copies.append(pltpu.make_async_copy(gram_v.at[bottom], gram_out.at[bottom], sem.at[3]))
    copies[-1].start()
    for copy in copies:
        copy.wait()


def on_device(tile_values, tile_rows, tile_cols, tile_depths, tile_live, factor_b, factor_c, proj):
    n_ia, n_ja, n_ka = (lax.axis_size(name) for name in ("ia", "ja", "ka"))
    owners = n_ja * n_ka
    slot_total, tile = tile_values.shape
    slots = slot_total // owners
    rank = factor_b.shape[0]
    columns = proj.shape[1]
    half = columns // 2
    height = half // owners
    chunks_b, chunks_c = n_ia * n_ka, n_ia * n_ja
    vmem, dma = pltpu.VMEM, pltpu.SemaphoreType.DMA
    f32, bf16, i32 = jnp.float32, jnp.bfloat16, jnp.int32
    held = pl.pallas_call(
        functools.partial(kernel, n_ia, n_ja, n_ka),
        out_shape=(
            vmem((ROWS_DEV, columns), f32),
            vmem((rank, ROWS_DEV), f32),
            vmem((3, owners, height, half), bf16),
        ),
        in_specs=[pl.BlockSpec(memory_space=pl.ANY)] * 8,
        out_specs=tuple([pl.BlockSpec(memory_space=pltpu.VMEM)] * 3),
        scratch_shapes=[
            vmem((slot_total, tile), bf16),
            vmem((slot_total, tile), i32),
            vmem((slot_total, tile), i32),
            vmem((slot_total, tile), i32),
            vmem(proj.shape, f32),
            pltpu.SMEM((1, owners), i32),
            vmem((slot_total, tile), f32),
            vmem((chunks_b, rank, LANES), bf16),
            vmem((chunks_c, rank, LANES), bf16),
            vmem((chunks_b, rank, LANES), f32),
            vmem((chunks_c, rank, LANES), f32),
            vmem((owners, slots, tile), i32),
            vmem((owners, slots, tile), i32),
            vmem((owners, slots, 2 * rank, tile), bf16),
            vmem((owners, slots, 2 * rank, tile), bf16),
            vmem((columns, slots * tile), bf16),
            vmem((columns, ROWS_DEV), f32),
            vmem((columns, 4 * ROWS_DEV), bf16),
            vmem((columns, 4 * ROWS_DEV), bf16),
            vmem((3, owners, height, half), f32),
            vmem((3, owners, height, half), bf16),
            vmem((3, owners, height, half), bf16),
            vmem((3, height, half), bf16),
            vmem((n_ia, 3, height, half), bf16),
            dma((8,)),
            dma((chunks_b,)), dma((chunks_b,)),
            dma((chunks_c,)), dma((chunks_c,)),
            dma((owners,)), dma((owners,)),
            dma((owners,)), dma((owners,)),
            dma((owners,)), dma((owners,)),
            dma((n_ia,)), dma((n_ia,)),
            dma((owners,)), dma((owners,)),
        ],
        compiler_params=pltpu.CompilerParams(collective_id=0, has_side_effects=True),
    )(
        tile_values, tile_rows, tile_cols, tile_depths, tile_live,
        factor_b[:, 0, :], factor_c[:, 0, :], proj,
    )
    return pl.pallas_call(
        finish,
        out_shape=(
            jax.ShapeDtypeStruct((ROWS_DEV, columns), f32),
            jax.ShapeDtypeStruct((columns, columns), f32),
            jax.ShapeDtypeStruct((rank, ROWS_DEV), f32),
        ),
        in_specs=[pl.BlockSpec(memory_space=pltpu.VMEM)] * 3,
        out_specs=tuple([pl.BlockSpec(memory_space=pl.ANY)] * 3),
        scratch_shapes=[vmem((columns, columns), f32), dma((4,))],
    )(*(pltpu.with_memory_space_constraint(array, vmem) for array in held))


def solution(mesh):
    return jax.shard_map(
        on_device,
        mesh=mesh,
        in_specs=(
            P(("ia", "ja", "ka"), None),
            P(("ia", "ja", "ka"), None),
            P(("ia", "ja", "ka"), None),
            P(("ia", "ja", "ka"), None),
            P(("ia", "ja", "ka"), None),
            P(None, "ja", ("ia", "ka")),
            P(None, "ka", ("ia", "ja")),
            P(),
        ),
        out_specs=(P(("ia", "ja", "ka"), None), P(), P(None, ("ia", "ja", "ka"))),
        check_vma=False,
    )
```
